32 devices in a mesh: groups: 2 (over y), seq: 4 (over z), mp: 2 (over x), sub: 2 (over core).
Axes of the slice: x: 2, y: 2, z: 4, core: 2. Of those that a mesh axis runs over, the one named last changes fastest.
Arguments:
- hidden_states: bfloat16 [2048, 8192], P(('groups', 'seq')), parts along dimension 0, may hold values from -8 to 8
- norm_gain: float32 [8192], replicated, may hold values from 0.25 to 1.75
- w_query: bfloat16 [8192, 2048], P('seq', ('mp', 'sub')), may hold values from -14 to 14
- w_keyval: bfloat16 [8192, 512], P('seq', ('mp', 'sub')), may hold values from -1 to 1
- doc_lengths: int32 [16], P('groups'), parts along dimension 0, may hold values from 1 to 512, 1024 in all
Outputs:
- attended: bfloat16 [2048, 2048], P(('groups', 'seq'), ('mp', 'sub')), parts along dimension 0
The draws below stay inside these ranges and needn't reach their ends.
There are 2 independent parts, one for each index of `groups`. The reference program is written for one: setup_inputs(seed, part) draws one part's arguments, and reference() takes and returns one part's arrays. A program takes and returns all parts, laid end to end along the dimension named above; an argument that names none is the same for every part. Nothing has to cross between parts.
Inputs may be any that keep to these rules, and one draw needn't show every extreme that they name: `doc_lengths`: the lengths sum to 1024 and the longest is exactly 512.
All inputs are finite; a program needn't handle non-finite values.
Results may differ from the reference program's by a relative error of at most 0.0079.
Values may be sent and summed in bfloat16 or wider, within the bound.
A program may use at most 64 MiB of HBM per device.

```python
import math
import jax
import jax.numpy as jnp
import numpy as np
from jax import lax

D = 8192
HEAD_DIM = 128
GROUP = 8
DOCS = 8
KV_HEADS = 2
Q_HEADS = 16
TOKENS = 1024


def projection_pair(key):
    factor = 1.0 / math.sqrt(D)
    keyval = jnp.clip(jax.random.normal(jax.random.fold_in(key, 11), (D, KV_HEADS, 2, HEAD_DIM), jnp.float32), -4.0, 4.0) * factor
    query_part = jnp.clip(jax.random.normal(jax.random.fold_in(key, 12), (D, Q_HEADS, HEAD_DIM), jnp.float32), -4.0, 4.0) * factor
    return (query_part.reshape(D, Q_HEADS * HEAD_DIM), keyval.reshape(D, 2 * KV_HEADS * HEAD_DIM))


def draw_w_query(key, part):
    return projection_pair(key)[0].astype(jnp.bfloat16)


def draw_w_keyval(key, part):
    return projection_pair(key)[1].astype(jnp.bfloat16)


def draw_hidden_states(key, part):
    drawn = jax.random.normal(jax.random.fold_in(key, 24), (TOKENS, D), jnp.float32)
    return jnp.clip(drawn, -6.0, 6.0).astype(jnp.bfloat16)


def profile(count, total, bound, slope):
    loads = [(1 << 20) // math.isqrt(rank ** slope) + 1 for rank in range(2, count + 1)]
    surplus, holding = total - bound - (count - 1), [1] * (count - 1)
    while surplus > 0:
        candidates = [i for i in range(count - 1) if holding[i] < bound]
        mass, left = sum([loads[i] for i in candidates]), surplus
        for i in candidates:
            addition = min(bound - holding[i], max(1, left * loads[i] // mass), surplus)
            holding[i] = holding[i] + addition
            surplus = surplus - addition
    return np.array([bound] + holding)


def uneven(own_key, number_of, total, reach, lean):
    if number_of == 2:
        one = jax.random.randint(own_key, (), max(1, total - reach), min(reach, total - 1) + 1)
        return jnp.stack([one, total - one])
    sizes = jnp.asarray(profile(number_of, total, reach, lean), jnp.int32)
    pairs = (number_of - 1) // 2
    source_of, receiver = sizes[1:1 + 2 * pairs:2], sizes[2:2 + 2 * pairs:2]
    slack = jnp.minimum(source_of - 1, reach - receiver)
    moved = jax.random.randint(jax.random.fold_in(own_key, 1), (pairs,), 0, 1 << 20) % (slack + 1)
    sizes = sizes.at[1:1 + 2 * pairs:2].set(source_of - moved).at[2:2 + 2 * pairs:2].set(receiver + moved)
    return sizes[jax.random.permutation(jax.random.fold_in(own_key, 2), number_of)]


def setup_inputs(seed: int = 0, part: int = 0) -> dict:
    key_list = jax.random.split(jax.random.key(seed), 6)
    own_keys = jax.random.split(jax.random.fold_in(key_list[5], part), 6)
    return {
        "hidden_states": draw_hidden_states(jax.random.fold_in(jax.random.fold_in(key_list[5], part), 71), part),
        "norm_gain": jnp.clip(1.0 + 0.15 * jax.random.normal(key_list[1], (D,), jnp.float32), 0.25, 1.75),
        "w_query": draw_w_query(jax.random.fold_in(key_list[5], 71), part),
        "w_keyval": draw_w_keyval(jax.random.fold_in(key_list[5], 71), part),
        "doc_lengths": uneven(own_keys[4], DOCS, TOKENS, TOKENS // 2, 2).astype(jnp.int32),
    }


NEG_LARGE = -1e+30
ROPE_BASE = 500000.0

def rms_norm(states, gain):
    as_float = states.astype(jnp.float32)
    factor = lax.rsqrt(lax.optimization_barrier(jnp.mean(as_float * as_float, axis=-1, keepdims=True)) + 1e-05)
    return (as_float * factor * gain[None, :].astype(jnp.float32)).astype(jnp.bfloat16)

def token_starts(positions, doc_lengths):
    doc_ends = jnp.cumsum(doc_lengths)
    begins = doc_ends - doc_lengths
    inside = begins[None, :] <= positions[:, None]
    return lax.optimization_barrier(jnp.max(jnp.where(inside, begins[None, :], 0), axis=1)).astype(jnp.int32)

def rope_tables(inner):
    half_dim = HEAD_DIM // 2
    frequency = jnp.exp(jnp.arange(half_dim, dtype=jnp.float32) * (-2.0 * math.log(ROPE_BASE) / HEAD_DIM))
    angle = inner.astype(jnp.float32)[:, None] * frequency[None, :]
    return (jnp.cos(angle)[:, None, :], jnp.sin(angle)[:, None, :])

def rotate(vectors, cosine, sine_table):
    half_dim = vectors.shape[-1] // 2
    first_half = vectors[..., :half_dim]
    second_half = vectors[..., half_dim:]
    return jnp.concatenate([first_half * cosine - second_half * sine_table, second_half * cosine + first_half * sine_table], axis=-1)

def reference(hidden_states, norm_gain, w_query, w_keyval, doc_lengths):
    positions = jnp.arange(TOKENS, dtype=jnp.int32)
    starts = token_starts(positions, doc_lengths)
    cosine, sine_table = rope_tables(positions - starts)
    normed = rms_norm(hidden_states, norm_gain)
    query_sum = jnp.dot(normed, w_query, preferred_element_type=jnp.float32)
    keyval_sum = jnp.dot(normed, w_keyval, preferred_element_type=jnp.float32)
    queries = rotate(query_sum.reshape(TOKENS, Q_HEADS, HEAD_DIM), cosine, sine_table).astype(jnp.bfloat16)
    paired = keyval_sum.reshape(TOKENS, KV_HEADS, 2, HEAD_DIM)
    keys = rotate(paired[:, :, 0, :], cosine, sine_table).astype(jnp.bfloat16)
    values = paired[:, :, 1, :].astype(jnp.bfloat16)
    allowed = (positions[None, :] >= starts[:, None]) & (positions[None, :] <= positions[:, None])
    softmax_scale = 1.0 / math.sqrt(HEAD_DIM)

    def one_head(head_index):
        kv_index = head_index // GROUP
        head_query = lax.dynamic_index_in_dim(queries, head_index, 1, keepdims=False)
        head_keys = lax.dynamic_index_in_dim(keys, kv_index, 1, keepdims=False)
        head_values = lax.dynamic_index_in_dim(values, kv_index, 1, keepdims=False)
        scores = jnp.dot(head_query, head_keys.T, preferred_element_type=jnp.float32) * softmax_scale
        scores = jnp.where(allowed, scores, NEG_LARGE)
        row_max = lax.optimization_barrier(jnp.max(scores, axis=-1, keepdims=True))
        exponent = jnp.where(allowed, jnp.exp(scores - row_max), 0.0)
        summed = jnp.dot(exponent.astype(jnp.bfloat16), head_values, preferred_element_type=jnp.float32)
        return (summed / lax.optimization_barrier(jnp.sum(exponent, axis=-1, keepdims=True))).astype(jnp.bfloat16)
    heads = lax.map(one_head, jnp.arange(Q_HEADS, dtype=jnp.int32))
    return jnp.transpose(heads, (1, 0, 2)).reshape(TOKENS, Q_HEADS * HEAD_DIM)
```

```python
import functools
import math

import jax
import jax.numpy as jnp
from jax import lax
from jax.experimental import pallas as pl
from jax.experimental.pallas import tpu as pltpu
from jax.sharding import PartitionSpec as P

HEAD_DIM = 128
NEG_LARGE = -1e30
ROPE_BASE = 500000.0
MESH = pl.DeviceIdType.MESH
LAG = 3
HALVES = 2
BF16 = jnp.bfloat16
F32 = jnp.float32


def repeat(count, body):
    if count <= 4:
        for step in range(count):
            body(step)
    else:
        lax.fori_loop(0, count, lambda step, carry: (body(step), carry)[1], 0)


def kernel(
    seq_n, mp_n,
    docs_ref, hidden_ref, gain_ref, wq_ref, wkv_ref, out_ref,
    hid, gain, weights, snd, act, kv_part, kv_tx, kv_rx, q_part, q_tx, q_rx, kvb, queries, starts_ref, cos_ref, sin_ref,
    local_sem, z_send, z_recv, m_send, m_recv, u_send, u_recv,
    kv_send, kv_recv, q_send, q_recv,
    ku_send, ku_recv, bias,
):
    seq, mp, sub = lax.axis_index("seq"), lax.axis_index("mp"), lax.axis_index("sub")
    other = 1 - sub
    _, _, parts, rows, depth = snd.shape
    piece_rows = parts * rows
    half_rows = piece_rows * mp_n * 2
    tokens = half_rows * HALVES
    first_row = (sub * mp_n + mp) * piece_rows
    heads = wq_ref.shape[1] // HEAD_DIM
    groups, wide = q_part.shape[2], q_part.shape[4]
    above = lax.rem(seq + 1, seq_n)
    below = lax.rem(seq + seq_n - 1, seq_n)

    longest = tokens * seq_n // 2
    back = min(seq_n - 1, -(-(longest - 1) // tokens))
    blocks = 2 * mp_n

    def hid_rows(row, count, sem):
        here = pl.ds(pl.multiple_of(row, rows), count)
        return pltpu.make_async_copy(
            hidden_ref.at[here, :], hid.at[here, :], local_sem.at[sem]
        )

    def piece_row(h, q):
        return h * half_rows + first_row + q * rows

    def hid_copy(h, q):
        return hid_rows(piece_row(h, q), rows, 3 + h * parts + q)

    def other_block(jump):
        return lax.rem(sub * mp_n + mp + jump, blocks)

    def hid_other(h, jump):
        return hid_rows(
            h * half_rows + other_block(jump) * piece_rows, piece_rows,
            3 + HALVES * parts + h * (blocks - 1) + jump - 1,
        )

    gain_copy = pltpu.make_async_copy(gain_ref, gain, local_sem.at[0])
    kv_copy = pltpu.make_async_copy(wkv_ref, weights.at[:, pl.ds(0, HEAD_DIM)], local_sem.at[1])
    q_copy = pltpu.make_async_copy(
        wq_ref, weights.at[:, pl.ds(HEAD_DIM, heads * HEAD_DIM)], local_sem.at[2]
    )
    pieces = [(h, q) for h in range(HALVES) for q in range(parts)]
    for h, q in pieces:
        hid_copy(h, q).start()
        if h == 0 and q == 0:
            gain_copy.start()
    kv_copy.start()
    q_copy.start()
    for h in range(HALVES):
        for jump in range(1, blocks):
            hid_other(h, jump).start()

    barrier = pltpu.get_barrier_semaphore()
    for step in range(1, seq_n):
        pl.semaphore_signal(
            barrier, 1, device_id={"seq": lax.rem(seq + step, seq_n)}, device_id_type=MESH
        )
    for step in range(1, mp_n):
        pl.semaphore_signal(
            barrier, 1, device_id={"mp": lax.rem(mp + step, mp_n)}, device_id_type=MESH
        )
    pl.semaphore_signal(barrier, 1, device_id={"sub": other}, device_id_type=MESH)

    def remote(src, dst, send, recv, where):
        return pltpu.make_async_remote_copy(
            src_ref=src, dst_ref=dst, send_sem=send, recv_sem=recv,
            device_id=where, device_id_type=MESH,
        )

    gain_copy.wait()

    def columns(d):
        return pl.ds(pl.multiple_of(d * depth, depth), depth)

    def z_copy(d, h, q):
        return remote(
            snd.at[d, h, q], act.at[h, seq, sub, mp, q], z_send.at[d], z_recv.at[seq, h, q],
            {"seq": d},
        )

    def row_factor(here):
        square = jnp.zeros((rows, 1), F32)
        for d in range(seq_n):
            x = hid[here, d * depth : (d + 1) * depth].astype(F32)
            square = square + jnp.sum(x * x, axis=-1, keepdims=True)
        return lax.rsqrt(square * (1.0 / hid.shape[1]) + 1e-05)

    def scaled(here, factor, d):
        x = hid[here, columns(d)].astype(F32)
        return (x * factor * gain[:, columns(d)]).astype(BF16)

    def share_piece(h, q):
        hid_copy(h, q).wait()
        here = pl.ds(pl.multiple_of(piece_row(h, q), rows), rows)
        factor = row_factor(here)
        if h == 0 and q == 0:
            pl.semaphore_wait(barrier, seq_n - 1 + mp_n - 1 + 1)

        def normed(d):
            return scaled(here, factor, d)

        def send_piece(step):
            far = seq_n - 1 - step
            up, down = seq + far, seq - far

            @pl.when(up < seq_n)
            def _():
                snd[up, h, q] = normed(up)
                z_copy(up, h, q).start()

            @pl.when(down >= 0)
            def _():
                snd[down, h, q] = normed(down)
                z_copy(down, h, q).start()

        repeat(seq_n - 1, send_piece)
        act[h, seq, sub, mp, q] = normed(seq)

    for h, q in pieces:
        share_piece(h, q)

    def own_rows(h):
        for jump in range(1, blocks):
            hid_other(h, jump).wait()

        def chunk(at, carry):
            block = other_block(1 + at // parts)
            q = lax.rem(at, parts)
            row = h * half_rows + block * piece_rows + q * rows
            here = pl.ds(pl.multiple_of(row, rows), rows)
            act[h, seq, block // mp_n, lax.rem(block, mp_n), q] = scaled(
                here, row_factor(here), seq
            )
            return carry

        lax.fori_loop(0, (blocks - 1) * parts, chunk, 0)

    lane = lax.broadcasted_iota(jnp.int32, (tokens, HEAD_DIM), 1)
    half = HEAD_DIM // 2
    low = lane < half
    frequency = jnp.exp(
        jnp.where(low, lane, lane - half).astype(F32) * (-2.0 * math.log(ROPE_BASE) / HEAD_DIM)
    )

    def tables(block):
        @pl.when((block <= seq) & (block >= seq - back))
        def _():
            position = block * tokens + lax.broadcasted_iota(jnp.int32, (tokens, HEAD_DIM), 0)
            start = jnp.zeros((tokens, HEAD_DIM), jnp.int32)
            begin = jnp.int32(0)
            for doc in range(docs_ref.shape[0]):
                start = jnp.where(position >= begin, jnp.maximum(start, begin), start)
                begin = begin + docs_ref[doc]
            starts_ref[...] = start
            angle = (position - start).astype(F32) * frequency
            cos_ref[block - seq + back] = jnp.cos(angle)
            sine = jnp.sin(angle)
            sin_ref[block - seq + back] = jnp.where(low, -sine, sine)


    def span(h):
        return slice(h * half_rows, (h + 1) * half_rows)

    def rotate(u, h):
        return u * cos_ref[back, span(h), :] + pltpu.roll(u, half, 1) * sin_ref[back, span(h), :]

    def source(step):
        if isinstance(step, int) and step == 0:
            return seq
        high, low = seq_n - step, step - 1
        high = jnp.where(high > seq, high, high - 1)
        low = jnp.where(low < seq, low, low + 1)
        found = jnp.where(seq * 2 < seq_n, high, low)
        return found if isinstance(step, int) else jnp.where(step == 0, seq, found)

    def m_copy(src, m, h, q):
        block = act.at[h, src, sub, mp, q]
        return remote(block, block, m_send.at[src, m], m_recv.at[src, mp, h, q], {"mp": m})

    def m_arrival(src, m, h, q):
        block = act.at[h, src, sub, m, q]
        return remote(block, block, m_send.at[src, m], m_recv.at[src, m, h, q], {"mp": m})

    def u_copy(src, m, h, q):
        block = act.at[h, src, sub, m, q]
        return remote(block, block, u_send.at[src, h], u_recv.at[src, h], {"sub": other})

    def relay(step, h, q):
        src = source(step)

        remote(
            snd.at[src, h, q], act.at[h, src, sub, mp, q], z_send.at[src],
            z_recv.at[src, h, q], {"seq": src},
        ).wait_recv()
        for jump in range(1, mp_n):
            m_copy(src, lax.rem(mp + jump, mp_n), h, q).start()
        u_copy(src, mp, h, q).start()

    def relay_mp(step, h, q):
        src = source(step)
        for jump in range(1, mp_n):
            m = lax.rem(mp + jump, mp_n)
            m_arrival(src, m, h, q).wait_recv()
            u_copy(src, m, h, q).start()

    def multiply(step, h):
        src = source(step)
        if not isinstance(step, int) or step > 0:
            share = act.at[h, src, other]
            remote(
                share, share, u_send.at[src, h], u_recv.at[src, h], {"sub": other}
            ).wait_recv()
        block = act[h, src].reshape(half_rows, depth)
        product = jnp.dot(block, weights[...], preferred_element_type=F32)
        kv_part[src, span(h), :] = product[:, :HEAD_DIM]
        for g in range(groups):
            q_part[h, src, g] = product[:, HEAD_DIM + g * wide : HEAD_DIM + (g + 1) * wide]

    def relay_all(h, q):
        repeat(seq_n - 1, lambda step: relay(step + 1, h, q))

    def relay_mp_all(h, q):
        repeat(seq_n - 1, lambda step: relay_mp(step + 1, h, q))

    def place(g, array_pair, h, d):
        return array_pair[0].at[d] if g is None else array_pair[1].at[h, d, g]

    def moved(g, h, d, slot, where):
        sent = slot if g is None else d
        return remote(
            place(g, (kv_tx, q_tx), h, sent), place(g, (kv_rx, q_rx), h, slot),
            place(g, (kv_send, q_send), h, sent), place(g, (kv_recv, q_recv), h, slot),
            {"seq": where},
        )

    def arrived(g, h, slot):
        moved(g, h, 0, slot, above).wait_recv()

    def send_sum(g, h, d, first, slot, where):
        got = slot if g is None else d
        own = place(g, (kv_part, q_part), h, d)
        out = place(g, (kv_tx, q_tx), h, got)
        came = place(g, (kv_rx, q_rx), h, got)

        @pl.when(jnp.logical_not(first))
        def _():
            arrived(g, h, got)
            out[...] = (own[...] + came[...].astype(F32)).astype(BF16)

        @pl.when(first)
        def _():
            out[...] = own[...].astype(BF16)

        moved(g, h, d, slot, where).start()

    def finish(g, h):
        own = place(g, (kv_part, q_part), h, seq)

        @pl.when(seq > 0)
        def _():
            arrived(g, h, seq)
            own[...] = own[...] + place(g, (kv_rx, q_rx), h, seq)[...].astype(F32)

        @pl.when(seq < seq_n - 1)
        def _():
            arrived(g, h, seq_n)
            own[...] = own[...] + place(g, (kv_rx, q_rx), h, seq_n)[...].astype(F32)

        total = own[...]
        per = wide // HEAD_DIM
        for head in range(per):
            queries[h, g * per + head] = rotate(
                total[:, head * HEAD_DIM : (head + 1) * HEAD_DIM], h
            ).astype(BF16)

    def keys_up(d):
        return (seq < seq_n - 1) & (seq + 1 <= d + back)

    def in_window(d):
        return (d <= seq) & (d >= seq - back)

    def finish_keys(d):
        own = kv_part.at[d]

        @pl.when((seq > 0) & jnp.logical_not(keys_up(d)))
        def _():
            arrived(None, 0, d)

        @pl.when((seq < seq_n - 1) & (d == seq))
        def _():
            arrived(None, 0, seq_n + d)

        @pl.when(seq > 0)
        def _():
            own[...] = own[...] + kv_rx[d].astype(F32)

        @pl.when(seq < seq_n - 1)
        def _():
            own[...] = own[...] + kv_rx[seq_n + d].astype(F32)

        total = own[...]
        turned = total * cos_ref[d - seq + back] + pltpu.roll(total, half, 1) * sin_ref[d - seq + back]
        kvb[sub, d - seq + back] = jnp.where(sub == 0, turned, total).astype(BF16)
        ku_copy(d).start()

    def ku_copy(b):
        block = kvb.at[sub, b - seq + back]
        return remote(block, block, ku_send.at[b], ku_recv.at[b], {"sub": other})

    def ku_arrival(b):
        block = kvb.at[other, b - seq + back]
        return remote(block, block, ku_send.at[b], ku_recv.at[b], {"sub": other})

    def wait_keys(step):
        @pl.when(in_window(step))
        def _():
            ku_arrival(step).wait_recv()

    scale = 1.0 / math.sqrt(HEAD_DIM)
    window = back + 1
    one_shot = window <= 4
    exponent = scale * math.log2(math.e)

    def reach(h):
        low_key = h * half_rows + back * tokens - (longest - 1)
        return max(low_key // HEAD_DIM * HEAD_DIM, 0), back * tokens + (h + 1) * half_rows

    def key_parts(h):
        first, last = reach(h)
        for slot_of in range(window):
            a, b = max(first - slot_of * tokens, 0), min(last - slot_of * tokens, tokens)
            if a < b:
                yield slot_of, a, b

    def allow(h):
        first, last = reach(h)
        shape = (half_rows, last - first)
        row = seq * tokens + h * half_rows + lax.broadcasted_iota(jnp.int32, shape, 0)
        key_position = (seq - back) * tokens + first + lax.broadcasted_iota(jnp.int32, shape, 1)
        allowed = (key_position >= starts_ref[span(h), 0:1]) & (key_position <= row)
        bias[h, :, : last - first] = jnp.where(allowed, 0.0, NEG_LARGE)

    def attend(head, h):
        query = queries[h, head]
        if one_shot:
            first, last = reach(h)
            scores = jnp.concatenate([
                lax.dot_general(
                    query, kvb[0, slot_of, a:b, :], (((1,), (1,)), ((), ())),
                    preferred_element_type=F32,
                )
                for slot_of, a, b in key_parts(h)
            ], axis=1) * exponent + bias[h, :, : last - first]
            weight = jnp.exp2(scores - jnp.max(scores, axis=-1, keepdims=True))
            total = jnp.sum(weight, axis=-1, keepdims=True)
            value = jnp.concatenate(
                [kvb[1, slot_of, a:b, :] for slot_of, a, b in key_parts(h)], axis=0
            )
            summed = jnp.dot(weight.astype(BF16), value, preferred_element_type=F32)
        else:
            shape = (half_rows, tokens)
            row = seq * tokens + h * half_rows + lax.broadcasted_iota(jnp.int32, shape, 0)
            column = lax.broadcasted_iota(jnp.int32, shape, 1)
            row_start = starts_ref[span(h), 0:1]

            def block(j, state):
                top, total, summed = state
                key_position = (seq - back + j) * tokens + column
                allowed = (key_position >= row_start) & (key_position <= row)
                scores = lax.dot_general(
                    query, kvb[0, j], (((1,), (1,)), ((), ())),
                    preferred_element_type=F32,
                ) * scale
                scores = jnp.where(allowed, scores, NEG_LARGE)
                new_top = jnp.maximum(top, jnp.max(scores, axis=-1, keepdims=True))
                weight = jnp.where(allowed, jnp.exp(scores - new_top), 0.0)
                rescale = jnp.exp(top - new_top)
                total = total * rescale + jnp.sum(weight, axis=-1, keepdims=True)
                summed = summed * rescale + jnp.dot(
                    weight.astype(BF16), kvb[1, j],
                    preferred_element_type=F32,
                )
                return new_top, total, summed

            _, total, summed = lax.fori_loop(
                jnp.maximum(back - seq, 0), window, block,
                (
                    jnp.full((half_rows, 1), NEG_LARGE, F32),
                    jnp.zeros((half_rows, 1), F32),
                    jnp.zeros((half_rows, HEAD_DIM), F32),
                ),
            )
        out_ref[span(h), head * HEAD_DIM : (head + 1) * HEAD_DIM] = (summed / total).astype(BF16)

    per_group = wide // HEAD_DIM

    def attend_group(g, h):
        for head in range(g * per_group, (g + 1) * per_group):
            attend(head, h)

    hops = seq_n - 1
    half_units = hops * groups
    units = half_units * HALVES + seq_n
    kinds = [(h, g) for h in range(HALVES) for g in range(groups)]

    def done_slot(node, h, g):
        up_rank, down_rank = hops - node, node
        if g is None:
            unit = half_units
        else:
            up_rank, down_rank = up_rank * groups, down_rank * groups
            unit = g + (half_units * h + seq_n if h > 0 else 0)
        return jnp.maximum(
            jnp.where(node > 0, unit + up_rank + LAG * node, 0),
            jnp.where(node < hops, unit + down_rank + LAG * (hops - node), 0),
        )

    def hop(unit, up):
        live = (unit >= 0) & (unit < units)
        unit = jnp.maximum(unit, 0)
        keyed = (unit >= half_units) & (unit < half_units + seq_n)
        k_rank = jnp.clip(unit - half_units, 0, hops)
        queried = jnp.where(unit < half_units, unit, jnp.maximum(unit - seq_n, 0))
        h = queried // half_units
        within = queried - h * half_units
        q_rank = within // groups
        g = within - q_rank * groups

        def go(d, g):
            if up:
                send_sum(g, h, d, seq == 0, d, above)
            else:
                slot = seq_n + d if g is None else jnp.where(seq - 1 == d, seq_n, d)
                send_sum(g, h, d, seq == hops, slot, below)

        def owner(rank):
            return hops - rank if up else rank

        def ahead(d):
            return (d > seq) if up else (d < seq)

        @pl.when(live & keyed & (keys_up(owner(k_rank)) if up else ahead(owner(k_rank))))
        def _():
            go(owner(k_rank), None)

        @pl.when(live & jnp.logical_not(keyed) & ahead(owner(q_rank)))
        def _():
            go(owner(q_rank), g)

    up_end = jnp.where(seq < hops, units + LAG * seq, 0)
    down_end = jnp.where(seq > 0, units + LAG * (hops - seq), 0)
    keys_end = half_units + 1 + jnp.maximum(
        hops - jnp.maximum(seq - back, 0) + LAG * seq, seq + LAG * (hops - seq)
    )
    quiet = jnp.maximum(jnp.maximum(up_end, down_end), keys_end)
    early = done_slot(seq, HALVES - 1, 0) < quiet

    def slot(t):
        hop(t - LAG * seq, True)
        hop(t - LAG * (hops - seq), False)
        for h, g in kinds:
            @pl.when(t == done_slot(seq, h, g))
            def _():
                finish(g, h)
                if h > 0:
                    if g == 0:
                        @pl.when(early)
                        def _():
                            repeat(seq_n, wait_keys)
                    attend_group(g, h)

        def keys(d):
            from_below = jnp.where(seq > 0, hops - d + LAG * seq, 0)
            from_above = jnp.where(seq < hops, d + LAG * (hops - seq), 0)

            @pl.when(in_window(d) & (t == half_units + jnp.maximum(from_below, from_above)))
            def _():
                finish_keys(d)

        repeat(seq_n, keys)

    def slots(first, last):
        lax.fori_loop(first, last, lambda t, carry: (slot(t), carry)[1], 0)

    def fill(j, carry):
        @pl.when(j < back - seq)
        def _():
            kvb[0, j] = jnp.zeros((tokens, HEAD_DIM), BF16)
            kvb[1, j] = jnp.zeros((tokens, HEAD_DIM), BF16)
        return carry

    own_rows(0)
    relay_all(0, 0)
    own_rows(1)
    lax.fori_loop(0, seq_n, lambda block, carry: (tables(block), carry)[1], 0)
    for q in range(1, parts):
        relay_all(0, q)
        relay_mp_all(0, q - 1)
    if one_shot:
        lax.fori_loop(0, back, fill, 0)
        for h in range(HALVES):
            allow(h)
    kv_copy.wait()
    q_copy.wait()
    multiply(0, 0)
    multiply(0, 1)

    def last_of(h):
        def body(step):
            relay_mp(step + 1, h, parts - 1)
            multiply(step + 1, h)

        repeat(hops, body)

    last_of(0)
    at = 0
    for q in range(parts):
        slots(at, at + half_units // (parts + 1))
        at = at + half_units // (parts + 1)
        relay_all(1, q)
        if q > 0:
            relay_mp_all(1, q - 1)
    slots(at, half_units)
    last_of(1)
    slots(half_units, quiet)

    @pl.when(jnp.logical_not(early))
    def _():
        repeat(seq_n, wait_keys)

    for g in range(groups):
        attend_group(g, 0)
    slots(quiet, units + LAG * hops + 1)

    def drain(step):
        @pl.when(step != seq)
        def _():
            block = snd.at[step]
            remote(
                block, block, z_send.at[step], z_recv.at[step, 0, 0], {"seq": step}
            ).wait_send()
            for h, g in kinds:
                moved(g, h, step, step, above).wait_send()

            for h in range(HALVES):
                own = act.at[h, step, sub, mp]
                for jump in range(1, mp_n):
                    m = lax.rem(mp + jump, mp_n)
                    remote(
                        own, own, m_send.at[step, m], m_recv.at[step, m, 0, 0], {"mp": m}
                    ).wait_send()
                shared = act.at[h, step, sub]
                remote(
                    shared, shared, u_send.at[step, h], u_recv.at[step, h], {"sub": other}
                ).wait_send()

        @pl.when(in_window(step))
        def _():
            ku_copy(step).wait_send()

        @pl.when(keys_up(step))
        def _():
            moved(None, 0, step, step, above).wait_send()

        @pl.when(step < seq)
        def _():
            moved(None, 0, step, seq_n + step, below).wait_send()

    repeat(seq_n, drain)


def shards(seq_n, mp_n, hidden_states, norm_gain, w_query, w_keyval, doc_lengths):
    tokens, width = hidden_states.shape
    depth, q_columns = w_query.shape
    heads = q_columns // HEAD_DIM
    wide = 2 * HEAD_DIM if heads % 2 == 0 else HEAD_DIM
    groups = q_columns // wide
    rows = 16
    half_rows = tokens // HALVES
    parts = half_rows // (mp_n * 2) // rows
    longest = tokens * seq_n // 2
    back = min(seq_n - 1, -(-(longest - 1) // tokens))
    keys = (back + 1) * tokens if back < 4 else HEAD_DIM
    dma = pltpu.SemaphoreType.DMA
    anywhere = pl.BlockSpec(memory_space=pl.ANY)
    return pl.pallas_call(
        functools.partial(kernel, seq_n, mp_n),
        out_shape=jax.ShapeDtypeStruct((tokens, q_columns), BF16),
        in_specs=[pl.BlockSpec(memory_space=pltpu.SMEM)] + [anywhere] * 4,
        out_specs=pl.BlockSpec(memory_space=pltpu.VMEM),
        scratch_shapes=[
            pltpu.VMEM((tokens, width), BF16),
            pltpu.VMEM((1, width), F32),
            pltpu.VMEM((depth, HEAD_DIM + q_columns), BF16),
            pltpu.VMEM((seq_n, HALVES, parts, rows, depth), BF16),
            pltpu.VMEM((HALVES, seq_n, 2, mp_n, parts, rows, depth), BF16),
            pltpu.VMEM((seq_n, tokens, HEAD_DIM), F32),
            pltpu.VMEM((2 * seq_n, tokens, HEAD_DIM), BF16),
            pltpu.VMEM((2 * seq_n, tokens, HEAD_DIM), BF16),
            pltpu.VMEM((HALVES, seq_n, groups, half_rows, wide), F32),
            pltpu.VMEM((HALVES, seq_n, groups, half_rows, wide), BF16),
            pltpu.VMEM((HALVES, seq_n + 1, groups, half_rows, wide), BF16),
            pltpu.VMEM((2, back + 1, tokens, HEAD_DIM), BF16),
            pltpu.VMEM((HALVES, heads, half_rows, HEAD_DIM), BF16),
            pltpu.VMEM((tokens, HEAD_DIM), jnp.int32),
            pltpu.VMEM((back + 1, tokens, HEAD_DIM), F32),
            pltpu.VMEM((back + 1, tokens, HEAD_DIM), F32),
            dma((3 + HALVES * (parts + 2 * mp_n - 1),)),
            dma((seq_n,)), dma((seq_n, HALVES, parts)),
            dma((seq_n, mp_n)), dma((seq_n, mp_n, HALVES, parts)),
            dma((seq_n, HALVES)), dma((seq_n, HALVES)),
            dma((2 * seq_n,)), dma((2 * seq_n,)),
            dma((HALVES, seq_n, groups)), dma((HALVES, seq_n + 1, groups)),
            dma((seq_n,)), dma((seq_n,)),
            pltpu.VMEM((HALVES, half_rows, keys), F32),
        ],
        compiler_params=pltpu.CompilerParams(
            collective_id=0, has_side_effects=True, vmem_limit_bytes=65000 * 1024
        ),
    )(doc_lengths, hidden_states, norm_gain[None, :], w_query, w_keyval)


def solution(mesh):
    in_specs = (
        P(("groups", "seq"), None),
        P(),
        P("seq", ("mp", "sub")),
        P("seq", ("mp", "sub")),
        P("groups"),
    )
    out_specs = P(("groups", "seq"), ("mp", "sub"))
    body = functools.partial(shards, mesh.shape["seq"], mesh.shape["mp"])
    return jax.shard_map(body, mesh=mesh, in_specs=in_specs, out_specs=out_specs, check_vma=False)
```

```python
import functools
import math

import jax
import jax.numpy as jnp
from jax import lax
from jax.experimental import pallas as pl
from jax.experimental.pallas import tpu as pltpu
from jax.sharding import PartitionSpec as P

HEAD_DIM = 128
NEG_LARGE = -1e30
ROPE_BASE = 500000.0
MESH = pl.DeviceIdType.MESH
LAG = 4
HALVES = 2
BF16 = jnp.bfloat16
F32 = jnp.float32


def repeat(count, body):
    if count <= 4:
        for step in range(count):
            body(step)
    else:
        lax.fori_loop(0, count, lambda step, carry: (body(step), carry)[1], 0)


def kernel(
    seq_n, mp_n,
    docs_ref, hidden_ref, gain_ref, wq_ref, wkv_ref, out_ref,
    hid, gain, weights, snd, act, kv_part, kv_tx, kv_rx, q_part, q_tx, q_rx, kvb, queries, starts_ref, cos_ref, sin_ref,
    local_sem, z_send, z_recv, m_send, m_recv, u_send, u_recv,
    kv_send, kv_recv, q_send, q_recv,
    ku_send, ku_recv, bias,
):
    seq, mp, sub = lax.axis_index("seq"), lax.axis_index("mp"), lax.axis_index("sub")
    other = 1 - sub
    _, _, parts, rows, depth = snd.shape
    piece_rows = parts * rows
    half_rows = piece_rows * mp_n * 2
    tokens = half_rows * HALVES
    first_row = (sub * mp_n + mp) * piece_rows
    heads = wq_ref.shape[1] // HEAD_DIM
    groups, wide = q_part.shape[2], q_part.shape[4]
    above = lax.rem(seq + 1, seq_n)
    below = lax.rem(seq + seq_n - 1, seq_n)

    longest = tokens * seq_n // 2
    back = min(seq_n - 1, -(-(longest - 1) // tokens))
    blocks = 2 * mp_n

    def hid_rows(row, count, sem):
        here = pl.ds(pl.multiple_of(row, rows), count)
        return pltpu.make_async_copy(
            hidden_ref.at[here, :], hid.at[here, :], local_sem.at[sem]
        )

    def piece_row(h, q):
        return h * half_rows + first_row + q * rows

    def hid_copy(h, q):
        return hid_rows(piece_row(h, q), rows, 3 + h * parts + q)

    def other_block(jump):
        return lax.rem(sub * mp_n + mp + jump, blocks)

    def hid_other(h, jump):
        return hid_rows(
            h * half_rows + other_block(jump) * piece_rows, piece_rows,
            3 + HALVES * parts + h * (blocks - 1) + jump - 1,
        )

    gain_copy = pltpu.make_async_copy(gain_ref, gain, local_sem.at[0])
    kv_copy = pltpu.make_async_copy(wkv_ref, weights.at[:, pl.ds(0, HEAD_DIM)], local_sem.at[1])
    q_copy = pltpu.make_async_copy(
        wq_ref, weights.at[:, pl.ds(HEAD_DIM, heads * HEAD_DIM)], local_sem.at[2]
    )
    pieces = [(h, q) for h in range(HALVES) for q in range(parts)]
    for h, q in pieces:
        hid_copy(h, q).start()
        if h == 0 and q == 0:
            gain_copy.start()
    kv_copy.start()
    q_copy.start()
    for h in range(HALVES):
        for jump in range(1, blocks):
            hid_other(h, jump).start()

    barrier = pltpu.get_barrier_semaphore()
    for step in range(1, seq_n):
        pl.semaphore_signal(
            barrier, 1, device_id={"seq": lax.rem(seq + step, seq_n)}, device_id_type=MESH
        )
    for step in range(1, mp_n):
        pl.semaphore_signal(
            barrier, 1, device_id={"mp": lax.rem(mp + step, mp_n)}, device_id_type=MESH
        )
    pl.semaphore_signal(barrier, 1, device_id={"sub": other}, device_id_type=MESH)

    def remote(src, dst, send, recv, where):
        return pltpu.make_async_remote_copy(
            src_ref=src, dst_ref=dst, send_sem=send, recv_sem=recv,
            device_id=where, device_id_type=MESH,
        )

    gain_copy.wait()

    def columns(d):
        return pl.ds(pl.multiple_of(d * depth, depth), depth)

    def z_copy(d, h, q):
        return remote(
            snd.at[d, h, q], act.at[h, seq, sub, mp, q], z_send.at[d], z_recv.at[seq, h, q],
            {"seq": d},
        )

    def row_factor(here):
        square = jnp.zeros((rows, 1), F32)
        for d in range(seq_n):
            x = hid[here, d * depth : (d + 1) * depth].astype(F32)
            square = square + jnp.sum(x * x, axis=-1, keepdims=True)
        return lax.rsqrt(square * (1.0 / hid.shape[1]) + 1e-05)

    def scaled(here, factor, d):
        x = hid[here, columns(d)].astype(F32)
        return (x * factor * gain[:, columns(d)]).astype(BF16)

    def share_piece(h, q, send):
        hid_copy(h, q).wait()
        here = pl.ds(pl.multiple_of(piece_row(h, q), rows), rows)
        factor = row_factor(here)
        if h == 0 and q == 0:
            pl.semaphore_wait(barrier, seq_n - 1 + mp_n - 1 + 1)

        def normed(d):
            return scaled(here, factor, d)

        def send_piece(step):
            far = seq_n - 1 - step
            up, down = seq + far, seq - far

            @pl.when(up < seq_n)
            def _():
                snd[up, h, q] = normed(up)
                if send:
                    z_copy(up, h, q).start()

            @pl.when(down >= 0)
            def _():
                snd[down, h, q] = normed(down)
                if send:
                    z_copy(down, h, q).start()

        repeat(seq_n - 1, send_piece)
        act[h, seq, sub, mp, q] = normed(seq)

    def send_later(h, q):
        def send_piece(step):
            far = seq_n - 1 - step
            up, down = seq + far, seq - far

            @pl.when(up < seq_n)
            def _():
                z_copy(up, h, q).start()

            @pl.when(down >= 0)
            def _():
                z_copy(down, h, q).start()

        repeat(seq_n - 1, send_piece)

    for at, (h, q) in enumerate(pieces):
        share_piece(h, q, at < 2)

    def own_rows(h):
        for jump in range(1, blocks):
            hid_other(h, jump).wait()

        def chunk(at, carry):
            block = other_block(1 + at // parts)
            q = lax.rem(at, parts)
            row = h * half_rows + block * piece_rows + q * rows
            here = pl.ds(pl.multiple_of(row, rows), rows)
            act[h, seq, block // mp_n, lax.rem(block, mp_n), q] = scaled(
                here, row_factor(here), seq
            )
            return carry

        lax.fori_loop(0, (blocks - 1) * parts, chunk, 0)

    lane = lax.broadcasted_iota(jnp.int32, (tokens, HEAD_DIM), 1)
    half = HEAD_DIM // 2
    low = lane < half
    frequency = jnp.exp(
        jnp.where(low, lane, lane - half).astype(F32) * (-2.0 * math.log(ROPE_BASE) / HEAD_DIM)
    )

    def tables(block):
        @pl.when((block <= seq) & (block >= seq - back))
        def _():
            position = block * tokens + lax.broadcasted_iota(jnp.int32, (tokens, HEAD_DIM), 0)
            start = jnp.zeros((tokens, HEAD_DIM), jnp.int32)
            begin = jnp.int32(0)
            for doc in range(docs_ref.shape[0]):
                start = jnp.where(position >= begin, jnp.maximum(start, begin), start)
                begin = begin + docs_ref[doc]
            starts_ref[...] = start
            angle = (position - start).astype(F32) * frequency
            cos_ref[block - seq + back] = jnp.cos(angle)
            sine = jnp.sin(angle)
            sin_ref[block - seq + back] = jnp.where(low, -sine, sine)


    def span(h):
        return slice(h * half_rows, (h + 1) * half_rows)

    def rotate(u, h):
        return u * cos_ref[back, span(h), :] + pltpu.roll(u, half, 1) * sin_ref[back, span(h), :]

    def source(step):
        if isinstance(step, int) and step == 0:
            return seq
        high, low = seq_n - step, step - 1
        high = jnp.where(high > seq, high, high - 1)
        low = jnp.where(low < seq, low, low + 1)
        found = jnp.where(seq * 2 < seq_n, high, low)
        return found if isinstance(step, int) else jnp.where(step == 0, seq, found)

    def m_copy(src, m, h, q):
        block = act.at[h, src, sub, mp, q]
        return remote(block, block, m_send.at[src, m], m_recv.at[src, mp, h, q], {"mp": m})

    def m_arrival(src, m, h, q):
        block = act.at[h, src, sub, m, q]
        return remote(block, block, m_send.at[src, m], m_recv.at[src, m, h, q], {"mp": m})

    def u_copy(src, m, h, q):
        block = act.at[h, src, sub, m, q]
        return remote(block, block, u_send.at[src, h], u_recv.at[src, h], {"sub": other})

    def relay(step, h, q):
        src = source(step)

        remote(
            snd.at[src, h, q], act.at[h, src, sub, mp, q], z_send.at[src],
            z_recv.at[src, h, q], {"seq": src},
        ).wait_recv()
        for jump in range(1, mp_n):
            m_copy(src, lax.rem(mp + jump, mp_n), h, q).start()
        u_copy(src, mp, h, q).start()

    def relay_mp(step, h, q):
        src = source(step)
        for jump in range(1, mp_n):
            m = lax.rem(mp + jump, mp_n)
            m_arrival(src, m, h, q).wait_recv()
            u_copy(src, m, h, q).start()

    def multiply(step, h):
        src = source(step)
        if not isinstance(step, int) or step > 0:
            share = act.at[h, src, other]
            remote(
                share, share, u_send.at[src, h], u_recv.at[src, h], {"sub": other}
            ).wait_recv()
        block = act[h, src].reshape(half_rows, depth)
        product = jnp.dot(block, weights[...], preferred_element_type=F32)
        kv_part[src, span(h), :] = product[:, :HEAD_DIM]
        for g in range(groups):
            q_part[h, src, g] = product[:, HEAD_DIM + g * wide : HEAD_DIM + (g + 1) * wide]

    def relay_all(h, q):
        repeat(seq_n - 1, lambda step: relay(step + 1, h, q))

    def relay_mp_all(h, q):
        repeat(seq_n - 1, lambda step: relay_mp(step + 1, h, q))

    def place(g, array_pair, h, d):
        if g is None:
            return array_pair[0].at[d, pl.ds(pl.multiple_of(h * half_rows, half_rows), half_rows), :]
        return array_pair[1].at[h, d, g]

    def sem(g, pair, h, d):
        return pair[0].at[h, d] if g is None else pair[1].at[h, d, g]

    def moved(g, h, d, slot, where):
        sent = slot if g is None else d
        return remote(
            place(g, (kv_tx, q_tx), h, sent), place(g, (kv_rx, q_rx), h, slot),
            sem(g, (kv_send, q_send), h, sent), sem(g, (kv_recv, q_recv), h, slot),
            {"seq": where},
        )

    def arrived(g, h, slot):
        moved(g, h, 0, slot, above).wait_recv()

    def send_sum(g, h, d, first, slot, where):
        got = slot if g is None else d
        own = place(g, (kv_part, q_part), h, d)
        out = place(g, (kv_tx, q_tx), h, got)
        came = place(g, (kv_rx, q_rx), h, got)

        @pl.when(jnp.logical_not(first))
        def _():
            arrived(g, h, got)
            out[...] = (own[...] + came[...].astype(F32)).astype(BF16)

        @pl.when(first)
        def _():
            out[...] = own[...].astype(BF16)

        moved(g, h, d, slot, where).start()

    def finish(g, h):
        own = place(g, (kv_part, q_part), h, seq)

        @pl.when(seq > 0)
        def _():
            arrived(g, h, seq)
            own[...] = own[...] + place(g, (kv_rx, q_rx), h, seq)[...].astype(F32)

        @pl.when(seq < seq_n - 1)
        def _():
            arrived(g, h, seq_n)
            own[...] = own[...] + place(g, (kv_rx, q_rx), h, seq_n)[...].astype(F32)

        total = own[...]
        per = wide // HEAD_DIM
        for head in range(per):
            queries[h, g * per + head] = rotate(
                total[:, head * HEAD_DIM : (head + 1) * HEAD_DIM], h
            ).astype(BF16)

    def keys_up(d):
        return (seq < seq_n - 1) & (seq + 1 <= d + back)

    def in_window(d):
        return (d <= seq) & (d >= seq - back)

    def finish_keys(d, h):
        own = place(None, (kv_part,), h, d)

        @pl.when((seq > 0) & jnp.logical_not(keys_up(d)))
        def _():
            arrived(None, h, d)

        @pl.when((seq < seq_n - 1) & (d == seq))
        def _():
            arrived(None, h, seq_n + d)

        @pl.when(seq > 0)
        def _():
            own[...] = own[...] + place(None, (kv_rx,), h, d)[...].astype(F32)

        @pl.when(seq < seq_n - 1)
        def _():
            own[...] = own[...] + place(None, (kv_rx,), h, seq_n + d)[...].astype(F32)

        total = own[...]
        slot_of = d - seq + back
        turned = (
            total * cos_ref[slot_of, span(h), :]
            + pltpu.roll(total, half, 1) * sin_ref[slot_of, span(h), :]
        )
        kvb[sub, slot_of, span(h), :] = jnp.where(sub == 0, turned, total).astype(BF16)
        ku_copy(d, h).start()

    def ku_copy(b, h):
        block = kvb.at[sub, b - seq + back, span(h), :]
        return remote(block, block, ku_send.at[h, b], ku_recv.at[h, b], {"sub": other})

    def ku_arrival(b, h):
        block = kvb.at[other, b - seq + back, span(h), :]
        return remote(block, block, ku_send.at[h, b], ku_recv.at[h, b], {"sub": other})

    def wait_keys(step):
        @pl.when(in_window(step))
        def _():
            for h in range(HALVES):
                ku_arrival(step, h).wait_recv()

    scale = 1.0 / math.sqrt(HEAD_DIM)
    window = back + 1
    one_shot = window <= 4
    exponent = scale * math.log2(math.e)

    def reach(h):
        low_key = h * half_rows + back * tokens - (longest - 1)
        return max(low_key // HEAD_DIM * HEAD_DIM, 0), back * tokens + (h + 1) * half_rows

    def key_parts(h):
        first, last = reach(h)
        for slot_of in range(window):
            a, b = max(first - slot_of * tokens, 0), min(last - slot_of * tokens, tokens)
            if a < b:
                yield slot_of, a, b

    def allow(h):
        first, last = reach(h)
        shape = (half_rows, last - first)
        row = seq * tokens + h * half_rows + lax.broadcasted_iota(jnp.int32, shape, 0)
        key_position = (seq - back) * tokens + first + lax.broadcasted_iota(jnp.int32, shape, 1)
        allowed = (key_position >= starts_ref[span(h), 0:1]) & (key_position <= row)
        bias[h, :, : last - first] = jnp.where(allowed, 0.0, NEG_LARGE)

    def attend(head, h):
        query = queries[h, head]
        if one_shot:
            first, last = reach(h)
            scores = jnp.concatenate([
                lax.dot_general(
                    query, kvb[0, slot_of, a:b, :], (((1,), (1,)), ((), ())),
                    preferred_element_type=F32,
                )
                for slot_of, a, b in key_parts(h)
            ], axis=1) * exponent + bias[h, :, : last - first]
            weight = jnp.exp2(scores - jnp.max(scores, axis=-1, keepdims=True))
            total = jnp.sum(weight, axis=-1, keepdims=True)
            value = jnp.concatenate(
                [kvb[1, slot_of, a:b, :] for slot_of, a, b in key_parts(h)], axis=0
            )
            summed = jnp.dot(weight.astype(BF16), value, preferred_element_type=F32)
        else:
            shape = (half_rows, tokens)
            row = seq * tokens + h * half_rows + lax.broadcasted_iota(jnp.int32, shape, 0)
            column = lax.broadcasted_iota(jnp.int32, shape, 1)
            row_start = starts_ref[span(h), 0:1]

            def block(j, state):
                top, total, summed = state
                key_position = (seq - back + j) * tokens + column
                allowed = (key_position >= row_start) & (key_position <= row)
                scores = lax.dot_general(
                    query, kvb[0, j], (((1,), (1,)), ((), ())),
                    preferred_element_type=F32,
                ) * scale
                scores = jnp.where(allowed, scores, NEG_LARGE)
                new_top = jnp.maximum(top, jnp.max(scores, axis=-1, keepdims=True))
                weight = jnp.where(allowed, jnp.exp(scores - new_top), 0.0)
                rescale = jnp.exp(top - new_top)
                total = total * rescale + jnp.sum(weight, axis=-1, keepdims=True)
                summed = summed * rescale + jnp.dot(
                    weight.astype(BF16), kvb[1, j],
                    preferred_element_type=F32,
                )
                return new_top, total, summed

            _, total, summed = lax.fori_loop(
                jnp.maximum(back - seq, 0), window, block,
                (
                    jnp.full((half_rows, 1), NEG_LARGE, F32),
                    jnp.zeros((half_rows, 1), F32),
                    jnp.zeros((half_rows, HEAD_DIM), F32),
                ),
            )
        out_ref[span(h), head * HEAD_DIM : (head + 1) * HEAD_DIM] = (summed / total).astype(BF16)

    per_group = wide // HEAD_DIM

    def attend_group(g, h):
        for head in range(g * per_group, (g + 1) * per_group):
            attend(head, h)

    hops = seq_n - 1
    half_units = hops * groups
    base_k = (half_units, half_units + seq_n)
    base_q = (0, base_k[1] + seq_n)
    units = base_q[1] + half_units
    kinds = [(h, g) for h in range(HALVES) for g in range(groups)]

    def done_slot(node, h, g):
        unit = base_q[h] + g
        return jnp.maximum(
            jnp.where(node > 0, unit + (hops - node) * groups + LAG * node, 0),
            jnp.where(node < hops, unit + node * groups + LAG * (hops - node), 0),
        )

    def hop(unit, up):
        late = unit >= base_k[1]
        h = jnp.where(late, 1, 0)
        keyed_at = unit - jnp.where(late, base_k[1], base_k[0])
        queried_at = unit - jnp.where(late, base_q[1], base_q[0])
        keyed = (keyed_at >= 0) & (keyed_at < seq_n)
        queried = (queried_at >= 0) & (queried_at < half_units)
        k_rank = jnp.clip(keyed_at, 0, hops)
        within = jnp.clip(queried_at, 0, half_units - 1)
        q_rank = within // groups
        g = within - q_rank * groups

        def go(d, g):
            if up:
                send_sum(g, h, d, seq == 0, d, above)
            else:
                slot = seq_n + d if g is None else jnp.where(seq - 1 == d, seq_n, d)
                send_sum(g, h, d, seq == hops, slot, below)

        def owner(rank):
            return hops - rank if up else rank

        def ahead(d):
            return (d > seq) if up else (d < seq)

        @pl.when(keyed & (keys_up(owner(k_rank)) if up else ahead(owner(k_rank))))
        def _():
            go(owner(k_rank), None)

        @pl.when(queried & ahead(owner(q_rank)))
        def _():
            go(owner(q_rank), g)

    up_end = jnp.where(seq < hops, units + LAG * seq, 0)
    down_end = jnp.where(seq > 0, units + LAG * (hops - seq), 0)
    keys_end = base_k[1] + 1 + jnp.maximum(
        hops - jnp.maximum(seq - back, 0) + LAG * seq, seq + LAG * (hops - seq)
    )
    quiet = jnp.maximum(jnp.maximum(up_end, down_end), keys_end)
    early = done_slot(seq, HALVES - 1, 0) < quiet

    def slot(t, halves):
        hop(t - LAG * seq, True)
        hop(t - LAG * (hops - seq), False)
        for h, g in kinds:
            if h in halves:
                @pl.when(t == done_slot(seq, h, g))
                def _():
                    finish(g, h)
                    if h > 0:
                        if g == 0:
                            @pl.when(early)
                            def _():
                                repeat(seq_n, wait_keys)
                        attend_group(g, h)

        def keys(d):
            from_below = jnp.where(seq > 0, hops - d + LAG * seq, 0)
            from_above = jnp.where(seq < hops, d + LAG * (hops - seq), 0)
            for h in halves:
                @pl.when(in_window(d) & (t == base_k[h] + jnp.maximum(from_below, from_above)))
                def _():
                    finish_keys(d, h)

        lax.fori_loop(0, seq_n, lambda d, carry: (keys(d), carry)[1], 0)

        if 1 in halves:
            @pl.when(t == quiet)
            def _():
                @pl.when(jnp.logical_not(early))
                def _():
                    repeat(seq_n, wait_keys)

                for g in range(groups):
                    attend_group(g, 0)

    def slots(first, last, halves):
        lax.fori_loop(first, last, lambda t, carry: (slot(t, halves), carry)[1], 0)

    def fill(j, carry):
        @pl.when(j < back - seq)
        def _():
            kvb[0, j] = jnp.zeros((tokens, HEAD_DIM), BF16)
            kvb[1, j] = jnp.zeros((tokens, HEAD_DIM), BF16)
        return carry

    def relay_piece(h, q):
        relay_all(h, q)
        at = pieces.index((h, q))
        if at + 2 < len(pieces):
            send_later(*pieces[at + 2])

    def last_of(h):
        def body(step):
            relay_mp(step + 1, h, parts - 1)
            multiply(step + 1, h)

        repeat(hops, body)

    own_rows(0)
    relay_piece(0, 0)
    own_rows(1)
    lax.fori_loop(0, seq_n, lambda block, carry: (tables(block), carry)[1], 0)
    for q in range(1, parts):
        relay_piece(0, q)
        relay_mp_all(0, q - 1)
    kv_copy.wait()
    q_copy.wait()
    multiply(0, 0)
    multiply(0, 1)
    if one_shot:
        lax.fori_loop(0, back, fill, 0)
        for h in range(HALVES):
            allow(h)
    last_of(0)
    at = 0
    for q in range(parts):
        upto = min(base_k[1] * (q + 1) * 3 // 10, base_k[1])
        slots(at, upto, (0,))
        at = upto
        relay_piece(1, q)
        if q > 0:
            relay_mp_all(1, q - 1)
    slots(at, base_k[1], (0,))
    last_of(1)
    slots(base_k[1], units + LAG * hops + 1, (0, 1))

    def drain(step):
        @pl.when(step != seq)
        def _():
            block = snd.at[step]
            remote(
                block, block, z_send.at[step], z_recv.at[step, 0, 0], {"seq": step}
            ).wait_send()
            for h, g in kinds:
                moved(g, h, step, step, above).wait_send()

            for h in range(HALVES):
                own = act.at[h, step, sub, mp]
                for jump in range(1, mp_n):
                    m = lax.rem(mp + jump, mp_n)
                    remote(
                        own, own, m_send.at[step, m], m_recv.at[step, m, 0, 0], {"mp": m}
                    ).wait_send()
                shared = act.at[h, step, sub]
                remote(
                    shared, shared, u_send.at[step, h], u_recv.at[step, h], {"sub": other}
                ).wait_send()

        for h in range(HALVES):
            @pl.when(in_window(step))
            def _():
                ku_copy(step, h).wait_send()

            @pl.when(keys_up(step))
            def _():
                moved(None, h, step, step, above).wait_send()

            @pl.when(step < seq)
            def _():
                moved(None, h, step, seq_n + step, below).wait_send()

    repeat(seq_n, drain)


def shards(seq_n, mp_n, hidden_states, norm_gain, w_query, w_keyval, doc_lengths):
    tokens, width = hidden_states.shape
    depth, q_columns = w_query.shape
    heads = q_columns // HEAD_DIM
    wide = 2 * HEAD_DIM if heads % 2 == 0 else HEAD_DIM
    groups = q_columns // wide
    rows = 16
    half_rows = tokens // HALVES
    parts = half_rows // (mp_n * 2) // rows
    longest = tokens * seq_n // 2
    back = min(seq_n - 1, -(-(longest - 1) // tokens))
    keys = (back + 1) * tokens if back < 4 else HEAD_DIM
    dma = pltpu.SemaphoreType.DMA
    anywhere = pl.BlockSpec(memory_space=pl.ANY)
    return pl.pallas_call(
        functools.partial(kernel, seq_n, mp_n),
        out_shape=jax.ShapeDtypeStruct((tokens, q_columns), BF16),
        in_specs=[pl.BlockSpec(memory_space=pltpu.SMEM)] + [anywhere] * 4,
        out_specs=pl.BlockSpec(memory_space=pltpu.VMEM),
        scratch_shapes=[
            pltpu.VMEM((tokens, width), BF16),
            pltpu.VMEM((1, width), F32),
            pltpu.VMEM((depth, HEAD_DIM + q_columns), BF16),
            pltpu.VMEM((seq_n, HALVES, parts, rows, depth), BF16),
            pltpu.VMEM((HALVES, seq_n, 2, mp_n, parts, rows, depth), BF16),
            pltpu.VMEM((seq_n, tokens, HEAD_DIM), F32),
            pltpu.VMEM((2 * seq_n, tokens, HEAD_DIM), BF16),
            pltpu.VMEM((2 * seq_n, tokens, HEAD_DIM), BF16),
            pltpu.VMEM((HALVES, seq_n, groups, half_rows, wide), F32),
            pltpu.VMEM((HALVES, seq_n, groups, half_rows, wide), BF16),
            pltpu.VMEM((HALVES, seq_n + 1, groups, half_rows, wide), BF16),
            pltpu.VMEM((2, back + 1, tokens, HEAD_DIM), BF16),
            pltpu.VMEM((HALVES, heads, half_rows, HEAD_DIM), BF16),
            pltpu.VMEM((tokens, HEAD_DIM), jnp.int32),
            pltpu.VMEM((back + 1, tokens, HEAD_DIM), F32),
            pltpu.VMEM((back + 1, tokens, HEAD_DIM), F32),
            dma((3 + HALVES * (parts + 2 * mp_n - 1),)),
            dma((seq_n,)), dma((seq_n, HALVES, parts)),
            dma((seq_n, mp_n)), dma((seq_n, mp_n, HALVES, parts)),
            dma((seq_n, HALVES)), dma((seq_n, HALVES)),
            dma((HALVES, 2 * seq_n)), dma((HALVES, 2 * seq_n)),
            dma((HALVES, seq_n, groups)), dma((HALVES, seq_n + 1, groups)),
            dma((HALVES, seq_n)), dma((HALVES, seq_n)),
            pltpu.VMEM((HALVES, half_rows, keys), F32),
        ],
        compiler_params=pltpu.CompilerParams(
            collective_id=0, has_side_effects=True, vmem_limit_bytes=65000 * 1024
        ),
    )(doc_lengths, hidden_states, norm_gain[None, :], w_query, w_keyval)


def solution(mesh):
    in_specs = (
        P(("groups", "seq"), None),
        P(),
        P("seq", ("mp", "sub")),
        P("seq", ("mp", "sub")),
        P("groups"),
    )
    out_specs = P(("groups", "seq"), ("mp", "sub"))
    body = functools.partial(shards, mesh.shape["seq"], mesh.shape["mp"])
    return jax.shard_map(body, mesh=mesh, in_specs=in_specs, out_specs=out_specs, check_vma=False)
```

```python
import functools
import math

import jax
import jax.numpy as jnp
from jax import lax
from jax.experimental import pallas as pl
from jax.experimental.pallas import tpu as pltpu
from jax.sharding import PartitionSpec as P

HEAD_DIM = 128
NEG_LARGE = -1e30
ROPE_BASE = 500000.0
MESH = pl.DeviceIdType.MESH
LAG = 4
HALVES = 2
BF16 = jnp.bfloat16
F32 = jnp.float32


def repeat(count, body):
    if count <= 4:
        for step in range(count):
            body(step)
    else:
        lax.fori_loop(0, count, lambda step, carry: (body(step), carry)[1], 0)


def kernel(
    seq_n, mp_n,
    docs_ref, hidden_ref, gain_ref, wq_ref, wkv_ref, out_ref,
    hid, gain, weights, snd, act, kv_part, kv_tx, kv_rx, q_part, q_tx, q_rx, kvb, queries, starts_ref, cos_ref, sin_ref,
    local_sem, z_send, z_recv, m_send, m_recv, u_send, u_recv,
    kv_send, kv_recv, q_send, q_recv,
    ku_send, ku_recv, bias, up_in, down_in,
):
    seq, mp, sub = lax.axis_index("seq"), lax.axis_index("mp"), lax.axis_index("sub")
    other = 1 - sub
    _, _, parts, rows, depth = snd.shape
    piece_rows = parts * rows
    half_rows = piece_rows * mp_n * 2
    tokens = half_rows * HALVES
    first_row = (sub * mp_n + mp) * piece_rows
    heads = wq_ref.shape[1] // HEAD_DIM
    groups, wide = q_part.shape[2], q_part.shape[4]
    above = lax.rem(seq + 1, seq_n)
    below = lax.rem(seq + seq_n - 1, seq_n)

    longest = tokens * seq_n // 2
    back = min(seq_n - 1, -(-(longest - 1) // tokens))
    blocks = 2 * mp_n

    def hid_rows(row, count, sem):
        here = pl.ds(pl.multiple_of(row, rows), count)
        return pltpu.make_async_copy(
            hidden_ref.at[here, :], hid.at[here, :], local_sem.at[sem]
        )

    def piece_row(h, q):
        return h * half_rows + first_row + q * rows

    def hid_copy(h, q):
        return hid_rows(piece_row(h, q), rows, 3 + h * parts + q)

    def other_block(jump):
        return lax.rem(sub * mp_n + mp + jump, blocks)

    def hid_other(h, jump):
        return hid_rows(
            h * half_rows + other_block(jump) * piece_rows, piece_rows,
            3 + HALVES * parts + h * (blocks - 1) + jump - 1,
        )

    gain_copy = pltpu.make_async_copy(gain_ref, gain, local_sem.at[0])
    kv_copy = pltpu.make_async_copy(wkv_ref, weights.at[:, pl.ds(0, HEAD_DIM)], local_sem.at[1])
    q_copy = pltpu.make_async_copy(
        wq_ref, weights.at[:, pl.ds(HEAD_DIM, heads * HEAD_DIM)], local_sem.at[2]
    )
    pieces = [(h, q) for h in range(HALVES) for q in range(parts)]
    for h, q in pieces:
        hid_copy(h, q).start()
        if h == 0 and q == 0:
            gain_copy.start()
    kv_copy.start()
    q_copy.start()
    for h in range(HALVES):
        for jump in range(1, blocks):
            hid_other(h, jump).start()

    barrier = pltpu.get_barrier_semaphore()

    @pl.when(seq > 0)
    def _():
        pl.semaphore_signal(barrier, 1, device_id={"seq": below}, device_id_type=MESH)

    @pl.when(seq < seq_n - 1)
    def _():
        pl.semaphore_signal(barrier, 1, device_id={"seq": above}, device_id_type=MESH)

    for step in range(1, mp_n):
        pl.semaphore_signal(
            barrier, 1, device_id={"mp": lax.rem(mp + step, mp_n)}, device_id_type=MESH
        )
    pl.semaphore_signal(barrier, 1, device_id={"sub": other}, device_id_type=MESH)

    def remote(src, dst, send, recv, where):
        return pltpu.make_async_remote_copy(
            src_ref=src, dst_ref=dst, send_sem=send, recv_sem=recv,
            device_id=where, device_id_type=MESH,
        )

    gain_copy.wait()

    def columns(d):
        return pl.ds(pl.multiple_of(d * depth, depth), depth)

    def z_copy(d, h, q):
        return remote(
            snd.at[d, h, q], act.at[h, seq, sub, mp, q], z_send.at[d], z_recv.at[seq, h, q],
            {"seq": d},
        )

    def row_factor(here):
        square = jnp.zeros((rows, 1), F32)
        for d in range(seq_n):
            x = hid[here, d * depth : (d + 1) * depth].astype(F32)
            square = square + jnp.sum(x * x, axis=-1, keepdims=True)
        return lax.rsqrt(square * (1.0 / hid.shape[1]) + 1e-05)

    def scaled(here, factor, d):
        x = hid[here, columns(d)].astype(F32)
        return (x * factor * gain[:, columns(d)]).astype(BF16)

    def tell(to, sem):
        pl.semaphore_signal(sem, 1, device_id={"seq": to}, device_id_type=MESH)

    def heard(sem):
        pl.semaphore_wait(sem, 1)

    def share_piece(h, q, send):
        hid_copy(h, q).wait()
        here = pl.ds(pl.multiple_of(piece_row(h, q), rows), rows)
        factor = row_factor(here)
        if h == 0 and q == 0:
            inner = (seq > 0) & (seq < seq_n - 1)
            pl.semaphore_wait(barrier, jnp.where(inner, 2, 1) + mp_n - 1 + 1)

            @pl.when(inner)
            def _():
                tell(below, up_in)
                tell(above, down_in)

        def normed(d):
            return scaled(here, factor, d)

        first = h == 0 and q == 0

        def send_piece(step):
            far = step + 1 if first else seq_n - 1 - step
            up, down = seq + far, seq - far
            if first:
                @pl.when((up < seq_n) & (step > 0))
                def _():
                    heard(up_in)
                    pl.when(seq > 0)(lambda: tell(below, up_in))

                @pl.when((down >= 0) & (step > 0))
                def _():
                    heard(down_in)
                    pl.when(seq < seq_n - 1)(lambda: tell(above, down_in))

            @pl.when(up < seq_n)
            def _():
                snd[up, h, q] = normed(up)
                if send:
                    z_copy(up, h, q).start()

            @pl.when(down >= 0)
            def _():
                snd[down, h, q] = normed(down)
                if send:
                    z_copy(down, h, q).start()

        repeat(seq_n - 1, send_piece)
        act[h, seq, sub, mp, q] = normed(seq)

    def send_later(h, q):
        def send_piece(step):
            far = seq_n - 1 - step
            up, down = seq + far, seq - far

            @pl.when(up < seq_n)
            def _():
                z_copy(up, h, q).start()

            @pl.when(down >= 0)
            def _():
                z_copy(down, h, q).start()

        repeat(seq_n - 1, send_piece)

    for at, (h, q) in enumerate(pieces):
        share_piece(h, q, at < 2)

    def own_rows(h):
        for jump in range(1, blocks):
            hid_other(h, jump).wait()

        def chunk(at, carry):
            block = other_block(1 + at // parts)
            q = lax.rem(at, parts)
            row = h * half_rows + block * piece_rows + q * rows
            here = pl.ds(pl.multiple_of(row, rows), rows)
            act[h, seq, block // mp_n, lax.rem(block, mp_n), q] = scaled(
                here, row_factor(here), seq
            )
            return carry

        lax.fori_loop(0, (blocks - 1) * parts, chunk, 0)

    lane = lax.broadcasted_iota(jnp.int32, (tokens, HEAD_DIM), 1)
    half = HEAD_DIM // 2
    low = lane < half
    frequency = jnp.exp(
        jnp.where(low, lane, lane - half).astype(F32) * (-2.0 * math.log(ROPE_BASE) / HEAD_DIM)
    )

    def tables(block):
        @pl.when((block <= seq) & (block >= seq - back))
        def _():
            position = block * tokens + lax.broadcasted_iota(jnp.int32, (tokens, HEAD_DIM), 0)
            start = jnp.zeros((tokens, HEAD_DIM), jnp.int32)
            begin = jnp.int32(0)
            for doc in range(docs_ref.shape[0]):
                start = jnp.where(position >= begin, jnp.maximum(start, begin), start)
                begin = begin + docs_ref[doc]
            starts_ref[...] = start
            angle = (position - start).astype(F32) * frequency
            cos_ref[block - seq + back] = jnp.cos(angle)
            sine = jnp.sin(angle)
            sin_ref[block - seq + back] = jnp.where(low, -sine, sine)


    def span(h):
        return slice(h * half_rows, (h + 1) * half_rows)

    def rotate(u, h):
        return u * cos_ref[back, span(h), :] + pltpu.roll(u, half, 1) * sin_ref[back, span(h), :]

    def source(step):
        if isinstance(step, int) and step == 0:
            return seq
        high, low = seq_n - step, step - 1
        high = jnp.where(high > seq, high, high - 1)
        low = jnp.where(low < seq, low, low + 1)
        found = jnp.where(seq * 2 < seq_n, high, low)
        return found if isinstance(step, int) else jnp.where(step == 0, seq, found)

    def m_copy(src, m, h, q):
        block = act.at[h, src, sub, mp, q]
        return remote(block, block, m_send.at[src, m], m_recv.at[src, mp, h, q], {"mp": m})

    def m_arrival(src, m, h, q):
        block = act.at[h, src, sub, m, q]
        return remote(block, block, m_send.at[src, m], m_recv.at[src, m, h, q], {"mp": m})

    def u_copy(src, m, h, q):
        block = act.at[h, src, sub, m, q]
        return remote(block, block, u_send.at[src, h], u_recv.at[src, h], {"sub": other})

    def relay(step, h, q):
        src = source(step)

        remote(
            snd.at[src, h, q], act.at[h, src, sub, mp, q], z_send.at[src],
            z_recv.at[src, h, q], {"seq": src},
        ).wait_recv()
        for jump in range(1, mp_n):
            m_copy(src, lax.rem(mp + jump, mp_n), h, q).start()
        u_copy(src, mp, h, q).start()

    def relay_mp(step, h, q):
        src = source(step)
        for jump in range(1, mp_n):
            m = lax.rem(mp + jump, mp_n)
            m_arrival(src, m, h, q).wait_recv()
            u_copy(src, m, h, q).start()

    def multiply(step, h):
        src = source(step)
        if not isinstance(step, int) or step > 0:
            share = act.at[h, src, other]
            remote(
                share, share, u_send.at[src, h], u_recv.at[src, h], {"sub": other}
            ).wait_recv()
        block = act[h, src].reshape(half_rows, depth)
        product = jnp.dot(block, weights[...], preferred_element_type=F32)
        kv_part[src, span(h), :] = product[:, :HEAD_DIM]
        for g in range(groups):
            q_part[h, src, g] = product[:, HEAD_DIM + g * wide : HEAD_DIM + (g + 1) * wide]

    def relay_all(h, q):
        repeat(seq_n - 1, lambda step: relay(step + 1, h, q))

    def relay_mp_all(h, q):
        repeat(seq_n - 1, lambda step: relay_mp(step + 1, h, q))

    def place(g, array_pair, h, d):
        if g is None:
            return array_pair[0].at[d, pl.ds(pl.multiple_of(h * half_rows, half_rows), half_rows), :]
        return array_pair[1].at[h, d, g]

    def sem(g, pair, h, d):
        return pair[0].at[h, d] if g is None else pair[1].at[h, d, g]

    def moved(g, h, d, slot, where):
        sent = slot if g is None else d
        return remote(
            place(g, (kv_tx, q_tx), h, sent), place(g, (kv_rx, q_rx), h, slot),
            sem(g, (kv_send, q_send), h, sent), sem(g, (kv_recv, q_recv), h, slot),
            {"seq": where},
        )

    def arrived(g, h, slot):
        moved(g, h, 0, slot, above).wait_recv()

    def send_sum(g, h, d, first, slot, where):
        got = slot if g is None else d
        own = place(g, (kv_part, q_part), h, d)
        out = place(g, (kv_tx, q_tx), h, got)
        came = place(g, (kv_rx, q_rx), h, got)

        @pl.when(jnp.logical_not(first))
        def _():
            arrived(g, h, got)
            out[...] = (own[...] + came[...].astype(F32)).astype(BF16)

        @pl.when(first)
        def _():
            out[...] = own[...].astype(BF16)

        moved(g, h, d, slot, where).start()

    def finish(g, h):
        own = place(g, (kv_part, q_part), h, seq)

        @pl.when(seq > 0)
        def _():
            arrived(g, h, seq)
            own[...] = own[...] + place(g, (kv_rx, q_rx), h, seq)[...].astype(F32)

        @pl.when(seq < seq_n - 1)
        def _():
            arrived(g, h, seq_n)
            own[...] = own[...] + place(g, (kv_rx, q_rx), h, seq_n)[...].astype(F32)

        total = own[...]
        per = wide // HEAD_DIM
        for head in range(per):
            queries[h, g * per + head] = rotate(
                total[:, head * HEAD_DIM : (head + 1) * HEAD_DIM], h
            ).astype(BF16)

    def keys_up(d):
        return (seq < seq_n - 1) & (seq + 1 <= d + back)

    def in_window(d):
        return (d <= seq) & (d >= seq - back)

    def finish_keys(d, h):
        own = place(None, (kv_part,), h, d)

        @pl.when((seq > 0) & jnp.logical_not(keys_up(d)))
        def _():
            arrived(None, h, d)

        @pl.when((seq < seq_n - 1) & (d == seq))
        def _():
            arrived(None, h, seq_n + d)

        @pl.when(seq > 0)
        def _():
            own[...] = own[...] + place(None, (kv_rx,), h, d)[...].astype(F32)

        @pl.when(seq < seq_n - 1)
        def _():
            own[...] = own[...] + place(None, (kv_rx,), h, seq_n + d)[...].astype(F32)

        total = own[...]
        slot_of = d - seq + back
        turned = (
            total * cos_ref[slot_of, span(h), :]
            + pltpu.roll(total, half, 1) * sin_ref[slot_of, span(h), :]
        )
        kvb[sub, slot_of, span(h), :] = jnp.where(sub == 0, turned, total).astype(BF16)
        ku_copy(d, h).start()

    def ku_copy(b, h):
        block = kvb.at[sub, b - seq + back, span(h), :]
        return remote(block, block, ku_send.at[h, b], ku_recv.at[h, b], {"sub": other})

    def ku_arrival(b, h):
        block = kvb.at[other, b - seq + back, span(h), :]
        return remote(block, block, ku_send.at[h, b], ku_recv.at[h, b], {"sub": other})

    def wait_keys(step):
        @pl.when(in_window(step))
        def _():
            for h in range(HALVES):
                ku_arrival(step, h).wait_recv()

    scale = 1.0 / math.sqrt(HEAD_DIM)
    window = back + 1
    one_shot = window <= 4
    exponent = scale * math.log2(math.e)

    def reach(h):
        low_key = h * half_rows + back * tokens - (longest - 1)
        return max(low_key // HEAD_DIM * HEAD_DIM, 0), back * tokens + (h + 1) * half_rows

    def key_parts(h):
        first, last = reach(h)
        for slot_of in range(window):
            a, b = max(first - slot_of * tokens, 0), min(last - slot_of * tokens, tokens)
            if a < b:
                yield slot_of, a, b

    def allow(h):
        first, last = reach(h)
        shape = (half_rows, last - first)
        row = seq * tokens + h * half_rows + lax.broadcasted_iota(jnp.int32, shape, 0)
        key_position = (seq - back) * tokens + first + lax.broadcasted_iota(jnp.int32, shape, 1)
        allowed = (key_position >= starts_ref[span(h), 0:1]) & (key_position <= row)
        bias[h, :, : last - first] = jnp.where(allowed, 0.0, NEG_LARGE)

    def attend(head, h):
        query = queries[h, head]
        if one_shot:
            first, last = reach(h)
            scores = jnp.concatenate([
                lax.dot_general(
                    query, kvb[0, slot_of, a:b, :], (((1,), (1,)), ((), ())),
                    preferred_element_type=F32,
                )
                for slot_of, a, b in key_parts(h)
            ], axis=1) * exponent + bias[h, :, : last - first]
            weight = jnp.exp2(scores - jnp.max(scores, axis=-1, keepdims=True))
            total = jnp.sum(weight, axis=-1, keepdims=True)
            value = jnp.concatenate(
                [kvb[1, slot_of, a:b, :] for slot_of, a, b in key_parts(h)], axis=0
            )
            summed = jnp.dot(weight.astype(BF16), value, preferred_element_type=F32)
        else:
            shape = (half_rows, tokens)
            row = seq * tokens + h * half_rows + lax.broadcasted_iota(jnp.int32, shape, 0)
            column = lax.broadcasted_iota(jnp.int32, shape, 1)
            row_start = starts_ref[span(h), 0:1]

            def block(j, state):
                top, total, summed = state
                key_position = (seq - back + j) * tokens + column
                allowed = (key_position >= row_start) & (key_position <= row)
                scores = lax.dot_general(
                    query, kvb[0, j], (((1,), (1,)), ((), ())),
                    preferred_element_type=F32,
                ) * scale
                scores = jnp.where(allowed, scores, NEG_LARGE)
                new_top = jnp.maximum(top, jnp.max(scores, axis=-1, keepdims=True))
                weight = jnp.where(allowed, jnp.exp(scores - new_top), 0.0)
                rescale = jnp.exp(top - new_top)
                total = total * rescale + jnp.sum(weight, axis=-1, keepdims=True)
                summed = summed * rescale + jnp.dot(
                    weight.astype(BF16), kvb[1, j],
                    preferred_element_type=F32,
                )
                return new_top, total, summed

            _, total, summed = lax.fori_loop(
                jnp.maximum(back - seq, 0), window, block,
                (
                    jnp.full((half_rows, 1), NEG_LARGE, F32),
                    jnp.zeros((half_rows, 1), F32),
                    jnp.zeros((half_rows, HEAD_DIM), F32),
                ),
            )
        out_ref[span(h), head * HEAD_DIM : (head + 1) * HEAD_DIM] = (summed / total).astype(BF16)

    per_group = wide // HEAD_DIM

    def attend_group(g, h):
        for head in range(g * per_group, (g + 1) * per_group):
            attend(head, h)

    hops = seq_n - 1
    half_units = hops * groups
    base_k = (half_units, half_units + seq_n)
    base_q = (0, base_k[1] + seq_n)
    units = base_q[1] + half_units
    kinds = [(h, g) for h in range(HALVES) for g in range(groups)]

    def done_slot(node, h, g):
        unit = base_q[h] + g
        return jnp.maximum(
            jnp.where(node > 0, unit + (hops - node) * groups + LAG * node, 0),
            jnp.where(node < hops, unit + node * groups + LAG * (hops - node), 0),
        )

    def hop(unit, up):
        late = unit >= base_k[1]
        h = jnp.where(late, 1, 0)
        keyed_at = unit - jnp.where(late, base_k[1], base_k[0])
        queried_at = unit - jnp.where(late, base_q[1], base_q[0])
        keyed = (keyed_at >= 0) & (keyed_at < seq_n)
        queried = (queried_at >= 0) & (queried_at < half_units)
        k_rank = jnp.clip(keyed_at, 0, hops)
        within = jnp.clip(queried_at, 0, half_units - 1)
        q_rank = within // groups
        g = within - q_rank * groups

        def go(d, g):
            if up:
                send_sum(g, h, d, seq == 0, d, above)
            else:
                slot = seq_n + d if g is None else jnp.where(seq - 1 == d, seq_n, d)
                send_sum(g, h, d, seq == hops, slot, below)

        def owner(rank):
            return hops - rank if up else rank

        def ahead(d):
            return (d > seq) if up else (d < seq)

        @pl.when(keyed & (keys_up(owner(k_rank)) if up else ahead(owner(k_rank))))
        def _():
            go(owner(k_rank), None)

        @pl.when(queried & ahead(owner(q_rank)))
        def _():
            go(owner(q_rank), g)

    up_end = jnp.where(seq < hops, units + LAG * seq, 0)
    down_end = jnp.where(seq > 0, units + LAG * (hops - seq), 0)
    keys_end = base_k[1] + 1 + jnp.maximum(
        hops - jnp.maximum(seq - back, 0) + LAG * seq, seq + LAG * (hops - seq)
    )
    quiet = jnp.maximum(jnp.maximum(up_end, down_end), keys_end)
    early = done_slot(seq, HALVES - 1, 0) < quiet

    def slot(t, halves):
        hop(t - LAG * seq, True)
        hop(t - LAG * (hops - seq), False)
        for h, g in kinds:
            if h in halves:
                @pl.when(t == done_slot(seq, h, g))
                def _():
                    finish(g, h)
                    if h > 0:
                        if g == 0:
                            @pl.when(early)
                            def _():
                                repeat(seq_n, wait_keys)
                        attend_group(g, h)

        def keys(d):
            from_below = jnp.where(seq > 0, hops - d + LAG * seq, 0)
            from_above = jnp.where(seq < hops, d + LAG * (hops - seq), 0)
            for h in halves:
                @pl.when(in_window(d) & (t == base_k[h] + jnp.maximum(from_below, from_above)))
                def _():
                    finish_keys(d, h)

        lax.fori_loop(0, seq_n, lambda d, carry: (keys(d), carry)[1], 0)

        if 1 in halves:
            @pl.when(t == quiet)
            def _():
                @pl.when(jnp.logical_not(early))
                def _():
                    repeat(seq_n, wait_keys)

                for g in range(groups):
                    attend_group(g, 0)

    def slots(first, last, halves):
        lax.fori_loop(first, last, lambda t, carry: (slot(t, halves), carry)[1], 0)

    def fill(j, carry):
        @pl.when(j < back - seq)
        def _():
            kvb[0, j] = jnp.zeros((tokens, HEAD_DIM), BF16)
            kvb[1, j] = jnp.zeros((tokens, HEAD_DIM), BF16)
        return carry

    def relay_piece(h, q):
        relay_all(h, q)
        at = pieces.index((h, q))
        if at + 2 < len(pieces):
            send_later(*pieces[at + 2])

    def last_of(h):
        def body(step):
            relay_mp(step + 1, h, parts - 1)
            multiply(step + 1, h)

        repeat(hops, body)

    own_rows(0)
    relay_piece(0, 0)
    own_rows(1)
    lax.fori_loop(0, seq_n, lambda block, carry: (tables(block), carry)[1], 0)
    for q in range(1, parts):
        relay_piece(0, q)
        relay_mp_all(0, q - 1)
    kv_copy.wait()
    q_copy.wait()
    multiply(0, 0)
    multiply(0, 1)
    if one_shot:
        lax.fori_loop(0, back, fill, 0)
        for h in range(HALVES):
            allow(h)
    last_of(0)
    at = 0
    for q in range(parts):
        upto = min(base_k[1] * (q + 1) * 3 // 10, base_k[1])
        slots(at, upto, (0,))
        at = upto
        relay_piece(1, q)
        if q > 0:
            relay_mp_all(1, q - 1)
    slots(at, base_k[1], (0,))
    def last_step(step, carry):
        relay_mp(step + 1, 1, parts - 1)
        multiply(step + 1, 1)
        slots(base_k[1] + step, base_k[1] + step + 1, (0,))
        return carry

    lax.fori_loop(0, hops, last_step, 0)
    slots(base_k[1] + hops, units + LAG * hops + 1, (0, 1))

    def drain(step):
        @pl.when(step != seq)
        def _():
            block = snd.at[step]
            remote(
                block, block, z_send.at[step], z_recv.at[step, 0, 0], {"seq": step}
            ).wait_send()
            for h, g in kinds:
                moved(g, h, step, step, above).wait_send()

            for h in range(HALVES):
                own = act.at[h, step, sub, mp]
                for jump in range(1, mp_n):
                    m = lax.rem(mp + jump, mp_n)
                    remote(
                        own, own, m_send.at[step, m], m_recv.at[step, m, 0, 0], {"mp": m}
                    ).wait_send()
                shared = act.at[h, step, sub]
                remote(
                    shared, shared, u_send.at[step, h], u_recv.at[step, h], {"sub": other}
                ).wait_send()

        for h in range(HALVES):
            @pl.when(in_window(step))
            def _():
                ku_copy(step, h).wait_send()

            @pl.when(keys_up(step))
            def _():
                moved(None, h, step, step, above).wait_send()

            @pl.when(step < seq)
            def _():
                moved(None, h, step, seq_n + step, below).wait_send()

    repeat(seq_n, drain)


def shards(seq_n, mp_n, hidden_states, norm_gain, w_query, w_keyval, doc_lengths):
    tokens, width = hidden_states.shape
    depth, q_columns = w_query.shape
    heads = q_columns // HEAD_DIM
    wide = 2 * HEAD_DIM if heads % 2 == 0 else HEAD_DIM
    groups = q_columns // wide
    rows = 16
    half_rows = tokens // HALVES
    parts = half_rows // (mp_n * 2) // rows
    longest = tokens * seq_n // 2
    back = min(seq_n - 1, -(-(longest - 1) // tokens))
    keys = (back + 1) * tokens if back < 4 else HEAD_DIM
    dma = pltpu.SemaphoreType.DMA
    anywhere = pl.BlockSpec(memory_space=pl.ANY)
    return pl.pallas_call(
        functools.partial(kernel, seq_n, mp_n),
        out_shape=jax.ShapeDtypeStruct((tokens, q_columns), BF16),
        in_specs=[pl.BlockSpec(memory_space=pltpu.SMEM)] + [anywhere] * 4,
        out_specs=pl.BlockSpec(memory_space=pltpu.VMEM),
        scratch_shapes=[
            pltpu.VMEM((tokens, width), BF16),
            pltpu.VMEM((1, width), F32),
            pltpu.VMEM((depth, HEAD_DIM + q_columns), BF16),
            pltpu.VMEM((seq_n, HALVES, parts, rows, depth), BF16),
            pltpu.VMEM((HALVES, seq_n, 2, mp_n, parts, rows, depth), BF16),
            pltpu.VMEM((seq_n, tokens, HEAD_DIM), F32),
            pltpu.VMEM((2 * seq_n, tokens, HEAD_DIM), BF16),
            pltpu.VMEM((2 * seq_n, tokens, HEAD_DIM), BF16),
            pltpu.VMEM((HALVES, seq_n, groups, half_rows, wide), F32),
            pltpu.VMEM((HALVES, seq_n, groups, half_rows, wide), BF16),
            pltpu.VMEM((HALVES, seq_n + 1, groups, half_rows, wide), BF16),
            pltpu.VMEM((2, back + 1, tokens, HEAD_DIM), BF16),
            pltpu.VMEM((HALVES, heads, half_rows, HEAD_DIM), BF16),
            pltpu.VMEM((tokens, HEAD_DIM), jnp.int32),
            pltpu.VMEM((back + 1, tokens, HEAD_DIM), F32),
            pltpu.VMEM((back + 1, tokens, HEAD_DIM), F32),
            dma((3 + HALVES * (parts + 2 * mp_n - 1),)),
            dma((seq_n,)), dma((seq_n, HALVES, parts)),
            dma((seq_n, mp_n)), dma((seq_n, mp_n, HALVES, parts)),
            dma((seq_n, HALVES)), dma((seq_n, HALVES)),
            dma((HALVES, 2 * seq_n)), dma((HALVES, 2 * seq_n)),
            dma((HALVES, seq_n, groups)), dma((HALVES, seq_n + 1, groups)),
            dma((HALVES, seq_n)), dma((HALVES, seq_n)),
            pltpu.VMEM((HALVES, half_rows, keys), F32),
            pltpu.SemaphoreType.REGULAR, pltpu.SemaphoreType.REGULAR,
        ],
        compiler_params=pltpu.CompilerParams(
            collective_id=0, has_side_effects=True, vmem_limit_bytes=65000 * 1024
        ),
    )(doc_lengths, hidden_states, norm_gain[None, :], w_query, w_keyval)


def solution(mesh):
    in_specs = (
        P(("groups", "seq"), None),
        P(),
        P("seq", ("mp", "sub")),
        P("seq", ("mp", "sub")),
        P("groups"),
    )
    out_specs = P(("groups", "seq"), ("mp", "sub"))
    body = functools.partial(shards, mesh.shape["seq"], mesh.shape["mp"])
    return jax.shard_map(body, mesh=mesh, in_specs=in_specs, out_specs=out_specs, check_vma=False)
```

```python
import functools
import math

import jax
import jax.numpy as jnp
from jax import lax
from jax.experimental import pallas as pl
from jax.experimental.pallas import tpu as pltpu
from jax.sharding import PartitionSpec as P

HEAD_DIM = 128
NEG_LARGE = -1e30
ROPE_BASE = 500000.0
MESH = pl.DeviceIdType.MESH
LAG = 5
HALVES = 2
BF16 = jnp.bfloat16
F32 = jnp.float32


def repeat(count, body):
    if count <= 4:
        for step in range(count):
            body(step)
    else:
        lax.fori_loop(0, count, lambda step, carry: (body(step), carry)[1], 0)


def kernel(
    seq_n, mp_n,
    docs_ref, hidden_ref, gain_ref, wq_ref, wkv_ref, out_ref,
    hid, gain, weights, snd, act, kv_part, kv_tx, kv_rx, q_part, q_tx, q_rx, kvb, queries, starts_ref, cos_ref, sin_ref,
    local_sem, z_send, z_recv, m_send, m_recv, u_send, u_recv,
    kv_send, kv_recv, q_send, q_recv,
    ku_send, ku_recv, bias, up_in, down_in,
):
    seq, mp, sub = lax.axis_index("seq"), lax.axis_index("mp"), lax.axis_index("sub")
    other = 1 - sub
    _, _, parts, rows, depth = snd.shape
    piece_rows = parts * rows
    half_rows = piece_rows * mp_n * 2
    tokens = half_rows * HALVES
    first_row = (sub * mp_n + mp) * piece_rows
    heads = wq_ref.shape[1] // HEAD_DIM
    groups, wide = q_part.shape[2], q_part.shape[4]
    above = lax.rem(seq + 1, seq_n)
    below = lax.rem(seq + seq_n - 1, seq_n)

    longest = tokens * seq_n // 2
    back = min(seq_n - 1, -(-(longest - 1) // tokens))
    blocks = 2 * mp_n

    def hid_rows(row, count, sem):
        here = pl.ds(pl.multiple_of(row, rows), count)
        return pltpu.make_async_copy(
            hidden_ref.at[here, :], hid.at[here, :], local_sem.at[sem]
        )

    def piece_row(h, q):
        return h * half_rows + first_row + q * rows

    def hid_copy(h, q):
        return hid_rows(piece_row(h, q), rows, 3 + h * parts + q)

    def other_block(jump):
        return lax.rem(sub * mp_n + mp + jump, blocks)

    def hid_other(h, jump):
        return hid_rows(
            h * half_rows + other_block(jump) * piece_rows, piece_rows,
            3 + HALVES * parts + h * (blocks - 1) + jump - 1,
        )

    gain_copy = pltpu.make_async_copy(gain_ref, gain, local_sem.at[0])
    kv_copy = pltpu.make_async_copy(wkv_ref, weights.at[:, pl.ds(0, HEAD_DIM)], local_sem.at[1])
    q_copy = pltpu.make_async_copy(
        wq_ref, weights.at[:, pl.ds(HEAD_DIM, heads * HEAD_DIM)], local_sem.at[2]
    )
    pieces = [(h, q) for h in range(HALVES) for q in range(parts)]
    for h, q in pieces:
        hid_copy(h, q).start()
        if h == 0 and q == 0:
            gain_copy.start()
    kv_copy.start()
    q_copy.start()
    for h in range(HALVES):
        for jump in range(1, blocks):
            hid_other(h, jump).start()

    barrier = pltpu.get_barrier_semaphore()

    @pl.when(seq > 0)
    def _():
        pl.semaphore_signal(barrier, 1, device_id={"seq": below}, device_id_type=MESH)

    @pl.when(seq < seq_n - 1)
    def _():
        pl.semaphore_signal(barrier, 1, device_id={"seq": above}, device_id_type=MESH)

    for step in range(1, mp_n):
        pl.semaphore_signal(
            barrier, 1, device_id={"mp": lax.rem(mp + step, mp_n)}, device_id_type=MESH
        )
    pl.semaphore_signal(barrier, 1, device_id={"sub": other}, device_id_type=MESH)

    def remote(src, dst, send, recv, where):
        return pltpu.make_async_remote_copy(
            src_ref=src, dst_ref=dst, send_sem=send, recv_sem=recv,
            device_id=where, device_id_type=MESH,
        )

    gain_copy.wait()

    def columns(d):
        return pl.ds(pl.multiple_of(d * depth, depth), depth)

    def z_copy(d, h, q):
        return remote(
            snd.at[d, h, q], act.at[h, seq, sub, mp, q], z_send.at[d], z_recv.at[seq, h, q],
            {"seq": d},
        )

    def row_factor(here):
        square = jnp.zeros((rows, 1), F32)
        for d in range(seq_n):
            x = hid[here, d * depth : (d + 1) * depth].astype(F32)
            square = square + jnp.sum(x * x, axis=-1, keepdims=True)
        return lax.rsqrt(square * (1.0 / hid.shape[1]) + 1e-05)

    def scaled(here, factor, d):
        x = hid[here, columns(d)].astype(F32)
        return (x * factor * gain[:, columns(d)]).astype(BF16)

    def tell(to, sem):
        pl.semaphore_signal(sem, 1, device_id={"seq": to}, device_id_type=MESH)

    def heard(sem):
        pl.semaphore_wait(sem, 1)

    def share_piece(h, q, send):
        hid_copy(h, q).wait()
        here = pl.ds(pl.multiple_of(piece_row(h, q), rows), rows)
        factor = row_factor(here)
        if h == 0 and q == 0:
            inner = (seq > 0) & (seq < seq_n - 1)
            pl.semaphore_wait(barrier, jnp.where(inner, 2, 1) + mp_n - 1 + 1)

            @pl.when(inner)
            def _():
                tell(below, up_in)
                tell(above, down_in)

        def normed(d):
            return scaled(here, factor, d)

        first = h == 0 and q == 0

        def send_piece(step):
            far = step + 1 if first else seq_n - 1 - step
            up, down = seq + far, seq - far
            if first:
                @pl.when((up < seq_n) & (step > 0))
                def _():
                    heard(up_in)
                    pl.when(seq > 0)(lambda: tell(below, up_in))

                @pl.when((down >= 0) & (step > 0))
                def _():
                    heard(down_in)
                    pl.when(seq < seq_n - 1)(lambda: tell(above, down_in))

            @pl.when(up < seq_n)
            def _():
                snd[up, h, q] = normed(up)
                if send:
                    z_copy(up, h, q).start()

            @pl.when(down >= 0)
            def _():
                snd[down, h, q] = normed(down)
                if send:
                    z_copy(down, h, q).start()

        repeat(seq_n - 1, send_piece)
        act[h, seq, sub, mp, q] = normed(seq)

    def send_later(h, q):
        def send_piece(step):
            far = seq_n - 1 - step
            up, down = seq + far, seq - far

            @pl.when(up < seq_n)
            def _():
                z_copy(up, h, q).start()

            @pl.when(down >= 0)
            def _():
                z_copy(down, h, q).start()

        repeat(seq_n - 1, send_piece)

    for at, (h, q) in enumerate(pieces):
        share_piece(h, q, at < 2)

    def own_rows(h):
        for jump in range(1, blocks):
            hid_other(h, jump).wait()

        def chunk(at, carry):
            block = other_block(1 + at // parts)
            q = lax.rem(at, parts)
            row = h * half_rows + block * piece_rows + q * rows
            here = pl.ds(pl.multiple_of(row, rows), rows)
            act[h, seq, block // mp_n, lax.rem(block, mp_n), q] = scaled(
                here, row_factor(here), seq
            )
            return carry

        lax.fori_loop(0, (blocks - 1) * parts, chunk, 0)

    lane = lax.broadcasted_iota(jnp.int32, (tokens, HEAD_DIM), 1)
    half = HEAD_DIM // 2
    low = lane < half
    frequency = jnp.exp(
        jnp.where(low, lane, lane - half).astype(F32) * (-2.0 * math.log(ROPE_BASE) / HEAD_DIM)
    )

    def tables(block):
        @pl.when((block <= seq) & (block >= seq - back))
        def _():
            position = block * tokens + lax.broadcasted_iota(jnp.int32, (tokens, HEAD_DIM), 0)
            start = jnp.zeros((tokens, HEAD_DIM), jnp.int32)
            begin = jnp.int32(0)
            for doc in range(docs_ref.shape[0]):
                start = jnp.where(position >= begin, jnp.maximum(start, begin), start)
                begin = begin + docs_ref[doc]
            starts_ref[...] = start
            angle = (position - start).astype(F32) * frequency
            cos_ref[block - seq + back] = jnp.cos(angle)
            sine = jnp.sin(angle)
            sin_ref[block - seq + back] = jnp.where(low, -sine, sine)


    def span(h):
        return slice(h * half_rows, (h + 1) * half_rows)

    def rotate(u, h):
        return u * cos_ref[back, span(h), :] + pltpu.roll(u, half, 1) * sin_ref[back, span(h), :]

    def source(step):
        if isinstance(step, int) and step == 0:
            return seq
        high, low = seq_n - step, step - 1
        high = jnp.where(high > seq, high, high - 1)
        low = jnp.where(low < seq, low, low + 1)
        found = jnp.where(seq * 2 < seq_n, high, low)
        return found if isinstance(step, int) else jnp.where(step == 0, seq, found)

    def m_copy(src, m, h, q):
        block = act.at[h, src, sub, mp, q]
        return remote(block, block, m_send.at[src, m], m_recv.at[src, mp, h, q], {"mp": m})

    def m_arrival(src, m, h, q):
        block = act.at[h, src, sub, m, q]
        return remote(block, block, m_send.at[src, m], m_recv.at[src, m, h, q], {"mp": m})

    def u_copy(src, m, h, q):
        block = act.at[h, src, sub, m, q]
        return remote(block, block, u_send.at[src, h], u_recv.at[src, h], {"sub": other})

    def relay(step, h, q):
        src = source(step)

        remote(
            snd.at[src, h, q], act.at[h, src, sub, mp, q], z_send.at[src],
            z_recv.at[src, h, q], {"seq": src},
        ).wait_recv()
        for jump in range(1, mp_n):
            m_copy(src, lax.rem(mp + jump, mp_n), h, q).start()
        u_copy(src, mp, h, q).start()

    def relay_mp(step, h, q):
        src = source(step)
        for jump in range(1, mp_n):
            m = lax.rem(mp + jump, mp_n)
            m_arrival(src, m, h, q).wait_recv()
            u_copy(src, m, h, q).start()

    def multiply(step, h):
        src = source(step)
        if not isinstance(step, int) or step > 0:
            share = act.at[h, src, other]
            remote(
                share, share, u_send.at[src, h], u_recv.at[src, h], {"sub": other}
            ).wait_recv()
        block = act[h, src].reshape(half_rows, depth)
        product = jnp.dot(block, weights[...], preferred_element_type=F32)
        kv_part[src, span(h), :] = product[:, :HEAD_DIM]
        for g in range(groups):
            q_part[h, src, g] = product[:, HEAD_DIM + g * wide : HEAD_DIM + (g + 1) * wide]

    def relay_all(h, q):
        repeat(seq_n - 1, lambda step: relay(step + 1, h, q))

    def relay_mp_all(h, q):
        repeat(seq_n - 1, lambda step: relay_mp(step + 1, h, q))

    def place(g, array_pair, h, d):
        if g is None:
            return array_pair[0].at[d, pl.ds(pl.multiple_of(h * half_rows, half_rows), half_rows), :]
        return array_pair[1].at[h, d, g]

    def sem(g, pair, h, d):
        return pair[0].at[h, d] if g is None else pair[1].at[h, d, g]

    def moved(g, h, d, slot, where):
        sent = slot if g is None else d
        return remote(
            place(g, (kv_tx, q_tx), h, sent), place(g, (kv_rx, q_rx), h, slot),
            sem(g, (kv_send, q_send), h, sent), sem(g, (kv_recv, q_recv), h, slot),
            {"seq": where},
        )

    def arrived(g, h, slot):
        moved(g, h, 0, slot, above).wait_recv()

    def send_sum(g, h, d, first, slot, where):
        got = slot if g is None else d
        own = place(g, (kv_part, q_part), h, d)
        out = place(g, (kv_tx, q_tx), h, got)
        came = place(g, (kv_rx, q_rx), h, got)

        @pl.when(jnp.logical_not(first))
        def _():
            arrived(g, h, got)
            out[...] = (own[...] + came[...].astype(F32)).astype(BF16)

        @pl.when(first)
        def _():
            out[...] = own[...].astype(BF16)

        moved(g, h, d, slot, where).start()

    def finish(g, h):
        own = place(g, (kv_part, q_part), h, seq)

        @pl.when(seq > 0)
        def _():
            arrived(g, h, seq)
            own[...] = own[...] + place(g, (kv_rx, q_rx), h, seq)[...].astype(F32)

        @pl.when(seq < seq_n - 1)
        def _():
            arrived(g, h, seq_n)
            own[...] = own[...] + place(g, (kv_rx, q_rx), h, seq_n)[...].astype(F32)

        total = own[...]
        per = wide // HEAD_DIM
        for head in range(per):
            queries[h, g * per + head] = rotate(
                total[:, head * HEAD_DIM : (head + 1) * HEAD_DIM], h
            ).astype(BF16)

    def keys_up(d):
        return (seq < seq_n - 1) & (seq + 1 <= d + back)

    def in_window(d):
        return (d <= seq) & (d >= seq - back)

    def finish_keys(d, h):
        own = place(None, (kv_part,), h, d)

        @pl.when((seq > 0) & jnp.logical_not(keys_up(d)))
        def _():
            arrived(None, h, d)

        @pl.when((seq < seq_n - 1) & (d == seq))
        def _():
            arrived(None, h, seq_n + d)

        @pl.when(seq > 0)
        def _():
            own[...] = own[...] + place(None, (kv_rx,), h, d)[...].astype(F32)

        @pl.when(seq < seq_n - 1)
        def _():
            own[...] = own[...] + place(None, (kv_rx,), h, seq_n + d)[...].astype(F32)

        total = own[...]
        slot_of = d - seq + back
        turned = (
            total * cos_ref[slot_of, span(h), :]
            + pltpu.roll(total, half, 1) * sin_ref[slot_of, span(h), :]
        )
        kvb[sub, slot_of, span(h), :] = jnp.where(sub == 0, turned, total).astype(BF16)
        ku_copy(d, h).start()

    def ku_copy(b, h):
        block = kvb.at[sub, b - seq + back, span(h), :]
        return remote(block, block, ku_send.at[h, b], ku_recv.at[h, b], {"sub": other})

    def ku_arrival(b, h):
        block = kvb.at[other, b - seq + back, span(h), :]
        return remote(block, block, ku_send.at[h, b], ku_recv.at[h, b], {"sub": other})

    def wait_keys(step):
        @pl.when(in_window(step))
        def _():
            for h in range(HALVES):
                ku_arrival(step, h).wait_recv()

    scale = 1.0 / math.sqrt(HEAD_DIM)
    window = back + 1
    one_shot = window <= 4
    exponent = scale * math.log2(math.e)

    def reach(h):
        low_key = h * half_rows + back * tokens - (longest - 1)
        return max(low_key // HEAD_DIM * HEAD_DIM, 0), back * tokens + (h + 1) * half_rows

    def key_parts(h):
        first, last = reach(h)
        for slot_of in range(window):
            a, b = max(first - slot_of * tokens, 0), min(last - slot_of * tokens, tokens)
            if a < b:
                yield slot_of, a, b

    def allow(h):
        first, last = reach(h)
        shape = (half_rows, last - first)
        row = seq * tokens + h * half_rows + lax.broadcasted_iota(jnp.int32, shape, 0)
        key_position = (seq - back) * tokens + first + lax.broadcasted_iota(jnp.int32, shape, 1)
        allowed = (key_position >= starts_ref[span(h), 0:1]) & (key_position <= row)
        bias[h, :, : last - first] = jnp.where(allowed, 0.0, NEG_LARGE)

    def attend(head, h):
        query = queries[h, head]
        if one_shot:
            first, last = reach(h)
            scores = jnp.concatenate([
                lax.dot_general(
                    query, kvb[0, slot_of, a:b, :], (((1,), (1,)), ((), ())),
                    preferred_element_type=F32,
                )
                for slot_of, a, b in key_parts(h)
            ], axis=1) * exponent + bias[h, :, : last - first]
            weight = jnp.exp2(scores - jnp.max(scores, axis=-1, keepdims=True))
            total = jnp.sum(weight, axis=-1, keepdims=True)
            value = jnp.concatenate(
                [kvb[1, slot_of, a:b, :] for slot_of, a, b in key_parts(h)], axis=0
            )
            summed = jnp.dot(weight.astype(BF16), value, preferred_element_type=F32)
        else:
            shape = (half_rows, tokens)
            row = seq * tokens + h * half_rows + lax.broadcasted_iota(jnp.int32, shape, 0)
            column = lax.broadcasted_iota(jnp.int32, shape, 1)
            row_start = starts_ref[span(h), 0:1]

            def block(j, state):
                top, total, summed = state
                key_position = (seq - back + j) * tokens + column
                allowed = (key_position >= row_start) & (key_position <= row)
                scores = lax.dot_general(
                    query, kvb[0, j], (((1,), (1,)), ((), ())),
                    preferred_element_type=F32,
                ) * scale
                scores = jnp.where(allowed, scores, NEG_LARGE)
                new_top = jnp.maximum(top, jnp.max(scores, axis=-1, keepdims=True))
                weight = jnp.where(allowed, jnp.exp(scores - new_top), 0.0)
                rescale = jnp.exp(top - new_top)
                total = total * rescale + jnp.sum(weight, axis=-1, keepdims=True)
                summed = summed * rescale + jnp.dot(
                    weight.astype(BF16), kvb[1, j],
                    preferred_element_type=F32,
                )
                return new_top, total, summed

            _, total, summed = lax.fori_loop(
                jnp.maximum(back - seq, 0), window, block,
                (
                    jnp.full((half_rows, 1), NEG_LARGE, F32),
                    jnp.zeros((half_rows, 1), F32),
                    jnp.zeros((half_rows, HEAD_DIM), F32),
                ),
            )
        out_ref[span(h), head * HEAD_DIM : (head + 1) * HEAD_DIM] = (summed / total).astype(BF16)

    per_group = wide // HEAD_DIM

    def attend_group(g, h):
        for head in range(g * per_group, (g + 1) * per_group):
            attend(head, h)

    hops = seq_n - 1
    half_units = hops * groups
    base_k = (half_units, half_units + seq_n)
    base_q = (0, base_k[1] + seq_n)
    units = base_q[1] + half_units
    kinds = [(h, g) for h in range(HALVES) for g in range(groups)]

    def done_slot(node, h, g):
        unit = base_q[h] + g
        return jnp.maximum(
            jnp.where(node > 0, unit + (hops - node) * groups + LAG * node, 0),
            jnp.where(node < hops, unit + node * groups + LAG * (hops - node), 0),
        )

    def hop(unit, up):
        late = unit >= base_k[1]
        h = jnp.where(late, 1, 0)
        keyed_at = unit - jnp.where(late, base_k[1], base_k[0])
        queried_at = unit - jnp.where(late, base_q[1], base_q[0])
        keyed = (keyed_at >= 0) & (keyed_at < seq_n)
        queried = (queried_at >= 0) & (queried_at < half_units)
        k_rank = jnp.clip(keyed_at, 0, hops)
        within = jnp.clip(queried_at, 0, half_units - 1)
        q_rank = within // groups
        g = within - q_rank * groups

        def go(d, g):
            if up:
                send_sum(g, h, d, seq == 0, d, above)
            else:
                slot = seq_n + d if g is None else jnp.where(seq - 1 == d, seq_n, d)
                send_sum(g, h, d, seq == hops, slot, below)

        def owner(rank):
            return hops - rank if up else rank

        def ahead(d):
            return (d > seq) if up else (d < seq)

        @pl.when(keyed & (keys_up(owner(k_rank)) if up else ahead(owner(k_rank))))
        def _():
            go(owner(k_rank), None)

        @pl.when(queried & ahead(owner(q_rank)))
        def _():
            go(owner(q_rank), g)

    up_end = jnp.where(seq < hops, units + LAG * seq, 0)
    down_end = jnp.where(seq > 0, units + LAG * (hops - seq), 0)
    keys_end = base_k[1] + 1 + jnp.maximum(
        hops - jnp.maximum(seq - back, 0) + LAG * seq, seq + LAG * (hops - seq)
    )
    quiet = jnp.maximum(jnp.maximum(up_end, down_end), keys_end)
    early = done_slot(seq, HALVES - 1, 0) < quiet

    def slot(t, halves):
        hop(t - LAG * seq, True)
        hop(t - LAG * (hops - seq), False)
        for h, g in kinds:
            if h in halves:
                @pl.when(t == done_slot(seq, h, g))
                def _():
                    finish(g, h)
                    if h > 0:
                        if g == 0:
                            @pl.when(early)
                            def _():
                                repeat(seq_n, wait_keys)
                        attend_group(g, h)

        def keys(d):
            from_below = jnp.where(seq > 0, hops - d + LAG * seq, 0)
            from_above = jnp.where(seq < hops, d + LAG * (hops - seq), 0)
            for h in halves:
                @pl.when(in_window(d) & (t == base_k[h] + jnp.maximum(from_below, from_above)))
                def _():
                    finish_keys(d, h)

        lax.fori_loop(0, seq_n, lambda d, carry: (keys(d), carry)[1], 0)

        if 1 in halves:
            @pl.when(t == quiet)
            def _():
                @pl.when(jnp.logical_not(early))
                def _():
                    repeat(seq_n, wait_keys)

                for g in range(groups):
                    attend_group(g, 0)

    def slots(first, last, halves):
        lax.fori_loop(first, last, lambda t, carry: (slot(t, halves), carry)[1], 0)

    def fill(j, carry):
        @pl.when(j < back - seq)
        def _():
            kvb[0, j] = jnp.zeros((tokens, HEAD_DIM), BF16)
            kvb[1, j] = jnp.zeros((tokens, HEAD_DIM), BF16)
        return carry

    def relay_piece(h, q):
        relay_all(h, q)
        at = pieces.index((h, q))
        if at + 2 < len(pieces):
            send_later(*pieces[at + 2])

    def last_of(h):
        def body(step):
            relay_mp(step + 1, h, parts - 1)
            multiply(step + 1, h)

        repeat(hops, body)

    own_rows(0)
    relay_piece(0, 0)
    own_rows(1)
    lax.fori_loop(0, seq_n, lambda block, carry: (tables(block), carry)[1], 0)
    for q in range(1, parts):
        relay_piece(0, q)
        relay_mp_all(0, q - 1)
    kv_copy.wait()
    q_copy.wait()
    multiply(0, 0)
    multiply(0, 1)
    if one_shot:
        lax.fori_loop(0, back, fill, 0)
        for h in range(HALVES):
            allow(h)
    last_of(0)
    at = 0
    for q in range(parts):
        upto = min(base_k[1] * (q + 1) * 3 // 10, base_k[1])
        slots(at, upto, (0,))
        at = upto
        relay_piece(1, q)
        if q > 0:
            relay_mp_all(1, q - 1)
    slots(at, base_k[1], (0,))
    def last_step(step, carry):
        relay_mp(step + 1, 1, parts - 1)
        multiply(step + 1, 1)
        slots(base_k[1] + step, base_k[1] + step + 1, (0,))
        return carry

    lax.fori_loop(0, hops, last_step, 0)
    slots(base_k[1] + hops, units + LAG * hops + 1, (0, 1))

    def drain(step):
        @pl.when(step != seq)
        def _():
            block = snd.at[step]
            remote(
                block, block, z_send.at[step], z_recv.at[step, 0, 0], {"seq": step}
            ).wait_send()
            for h, g in kinds:
                moved(g, h, step, step, above).wait_send()

            for h in range(HALVES):
                own = act.at[h, step, sub, mp]
                for jump in range(1, mp_n):
                    m = lax.rem(mp + jump, mp_n)
                    remote(
                        own, own, m_send.at[step, m], m_recv.at[step, m, 0, 0], {"mp": m}
                    ).wait_send()
                shared = act.at[h, step, sub]
                remote(
                    shared, shared, u_send.at[step, h], u_recv.at[step, h], {"sub": other}
                ).wait_send()

        for h in range(HALVES):
            @pl.when(in_window(step))
            def _():
                ku_copy(step, h).wait_send()

            @pl.when(keys_up(step))
            def _():
                moved(None, h, step, step, above).wait_send()

            @pl.when(step < seq)
            def _():
                moved(None, h, step, seq_n + step, below).wait_send()

    repeat(seq_n, drain)


def shards(seq_n, mp_n, hidden_states, norm_gain, w_query, w_keyval, doc_lengths):
    tokens, width = hidden_states.shape
    depth, q_columns = w_query.shape
    heads = q_columns // HEAD_DIM
    wide = 2 * HEAD_DIM if heads % 2 == 0 else HEAD_DIM
    groups = q_columns // wide
    rows = 16
    half_rows = tokens // HALVES
    parts = half_rows // (mp_n * 2) // rows
    longest = tokens * seq_n // 2
    back = min(seq_n - 1, -(-(longest - 1) // tokens))
    keys = (back + 1) * tokens if back < 4 else HEAD_DIM
    dma = pltpu.SemaphoreType.DMA
    anywhere = pl.BlockSpec(memory_space=pl.ANY)
    return pl.pallas_call(
        functools.partial(kernel, seq_n, mp_n),
        out_shape=jax.ShapeDtypeStruct((tokens, q_columns), BF16),
        in_specs=[pl.BlockSpec(memory_space=pltpu.SMEM)] + [anywhere] * 4,
        out_specs=pl.BlockSpec(memory_space=pltpu.VMEM),
        scratch_shapes=[
            pltpu.VMEM((tokens, width), BF16),
            pltpu.VMEM((1, width), F32),
            pltpu.VMEM((depth, HEAD_DIM + q_columns), BF16),
            pltpu.VMEM((seq_n, HALVES, parts, rows, depth), BF16),
            pltpu.VMEM((HALVES, seq_n, 2, mp_n, parts, rows, depth), BF16),
            pltpu.VMEM((seq_n, tokens, HEAD_DIM), F32),
            pltpu.VMEM((2 * seq_n, tokens, HEAD_DIM), BF16),
            pltpu.VMEM((2 * seq_n, tokens, HEAD_DIM), BF16),
            pltpu.VMEM((HALVES, seq_n, groups, half_rows, wide), F32),
            pltpu.VMEM((HALVES, seq_n, groups, half_rows, wide), BF16),
            pltpu.VMEM((HALVES, seq_n + 1, groups, half_rows, wide), BF16),
            pltpu.VMEM((2, back + 1, tokens, HEAD_DIM), BF16),
            pltpu.VMEM((HALVES, heads, half_rows, HEAD_DIM), BF16),
            pltpu.VMEM((tokens, HEAD_DIM), jnp.int32),
            pltpu.VMEM((back + 1, tokens, HEAD_DIM), F32),
            pltpu.VMEM((back + 1, tokens, HEAD_DIM), F32),
            dma((3 + HALVES * (parts + 2 * mp_n - 1),)),
            dma((seq_n,)), dma((seq_n, HALVES, parts)),
            dma((seq_n, mp_n)), dma((seq_n, mp_n, HALVES, parts)),
            dma((seq_n, HALVES)), dma((seq_n, HALVES)),
            dma((HALVES, 2 * seq_n)), dma((HALVES, 2 * seq_n)),
            dma((HALVES, seq_n, groups)), dma((HALVES, seq_n + 1, groups)),
            dma((HALVES, seq_n)), dma((HALVES, seq_n)),
            pltpu.VMEM((HALVES, half_rows, keys), F32),
            pltpu.SemaphoreType.REGULAR, pltpu.SemaphoreType.REGULAR,
        ],
        compiler_params=pltpu.CompilerParams(
            collective_id=0, has_side_effects=True, vmem_limit_bytes=65000 * 1024
        ),
    )(doc_lengths, hidden_states, norm_gain[None, :], w_query, w_keyval)


def solution(mesh):
    in_specs = (
        P(("groups", "seq"), None),
        P(),
        P("seq", ("mp", "sub")),
        P("seq", ("mp", "sub")),
        P("groups"),
    )
    out_specs = P(("groups", "seq"), ("mp", "sub"))
    body = functools.partial(shards, mesh.shape["seq"], mesh.shape["mp"])
    return jax.shard_map(body, mesh=mesh, in_specs=in_specs, out_specs=out_specs, check_vma=False)
```
